512 devices in a mesh: frame: 16 (over z_hi, x, core), tile: 32 (over z_lo, y).
Axes of the slice: x: 4, y: 4, z: 16 (z_hi: 2, z_lo: 8; z = z_hi * 8 + z_lo), core: 2. Of those that a mesh axis runs over, the one named last changes fastest.
Arguments:
- state_tokens: bfloat16 [16, 32768, 256], P('frame', 'tile'), may hold values from -12 to 12
- gain_time: float32 [256], replicated, may hold values from 0.25 to 1.75
- query_time: bfloat16 [256, 256], replicated, may hold values from -2 to 2
- key_time: bfloat16 [256, 256], replicated, may hold values from -2 to 2
- value_time: bfloat16 [256, 256], replicated, may hold values from -0.375 to 0.375
- output_time: bfloat16 [256, 256], replicated, may hold values from -0.375 to 0.375
- gain_space: float32 [256], replicated, may hold values from 0.25 to 1.75
- query_space: bfloat16 [256, 256], replicated, may hold values from -2 to 2
- key_space: bfloat16 [256, 256], replicated, may hold values from -2 to 2
- value_space: bfloat16 [256, 256], replicated, may hold values from -0.375 to 0.375
- output_space: bfloat16 [256, 256], replicated, may hold values from -0.375 to 0.375
- neighbours: int32 [256, 9], P('tile'), may hold values from -1 to 255, as said below
Outputs:
- updated: bfloat16 [16, 32768, 256], P('frame', 'tile')
The draws below stay inside these ranges and needn't reach their ends.
Inputs may be any that keep to these rules, and one draw needn't show every extreme that they name: `neighbours`: entry 0 of row b is b itself; the other entries are distinct block ids at most 8 blocks away from b in the cyclic order of the 256 blocks, or -1; only the last entry is ever -1.
All inputs are finite; a program needn't handle non-finite values.
Results may differ from the reference program's by a relative error of at most 0.013.
Values may be sent and summed in bfloat16 or wider, within the bound.
A program may use at most 64 MiB of HBM per device.

```python
import math
import jax
import jax.numpy as jnp
from jax import lax

WIDTH = 256
HEADS = 8
FRAMES = 16
BLOCK = 128
NEIGHBOUR_COUNT = 9
TOK_DEV = 1024
TOKENS = 32768
BLOCKS_DEV = 8
BLOCKS = 256


def draw_state_tokens(key, part):
    second = jax.random.fold_in(key, 102)
    values = jax.random.normal(second, (FRAMES, TOKENS, WIDTH), jnp.float32)
    return jnp.clip(values, -12.0, 12.0).astype(jnp.bfloat16)


def query_key_pair(key, tag):
    query_matrix = jax.random.normal(jax.random.fold_in(key, 200 + tag), (WIDTH, WIDTH), jnp.float32) / math.sqrt(WIDTH)
    key_matrix = jax.random.normal(jax.random.fold_in(key, 210 + tag), (WIDTH, WIDTH), jnp.float32) / math.sqrt(WIDTH)
    return (jnp.clip(query_matrix, -2.0, 2.0), jnp.clip(key_matrix, -2.0, 2.0))


def draw_query_time(key, part):
    return query_key_pair(key, 0)[0].astype(jnp.bfloat16)


def draw_key_time(key, part):
    return query_key_pair(key, 0)[1].astype(jnp.bfloat16)


def draw_query_space(key, part):
    return query_key_pair(key, 1)[0].astype(jnp.bfloat16)


def draw_key_space(key, part):
    return query_key_pair(key, 1)[1].astype(jnp.bfloat16)


def draw_neighbours(key, part):
    count = 2 * BLOCKS_DEV
    offsets = jnp.concatenate([jnp.arange(-BLOCKS_DEV, 0, dtype=jnp.int32), jnp.arange(1, BLOCKS_DEV + 1, dtype=jnp.int32)])
    scores = jax.random.randint(jax.random.fold_in(key, 301), (BLOCKS, count), 0, 1 << 20) * count + jnp.arange(count, dtype=jnp.int32)[None, :]
    chosen_values, picked = lax.top_k(scores, NEIGHBOUR_COUNT - 1)
    chosen = offsets[picked]
    block_ids = jnp.arange(BLOCKS, dtype=jnp.int32)[:, None] + jnp.concatenate([jnp.zeros((BLOCKS, 1), jnp.int32), chosen], axis=1)
    block_ids = block_ids % BLOCKS
    corner = jax.random.randint(jax.random.fold_in(key, 302), (BLOCKS,), 0, 6) == 0
    block_ids = block_ids.at[:, NEIGHBOUR_COUNT - 1].set(jnp.where(corner, -1, block_ids[:, NEIGHBOUR_COUNT - 1]))
    return block_ids.astype(jnp.int32)


def bell_draw(rng, dims, scale, bound, held_as=jnp.bfloat16):
    entries = scale * jax.random.normal(rng, dims, jnp.float32)
    return jnp.clip(entries, min=-bound, max=bound).astype(held_as)


def setup_inputs(seed: int = 0) -> dict:
    key_list = jax.random.split(jax.random.key(seed), 13)
    return {
        "state_tokens": draw_state_tokens(jax.random.fold_in(key_list[12], 71), 0),
        "gain_time": jnp.clip(1.0 + 0.15 * jax.random.normal(key_list[1], (WIDTH,), jnp.float32), 0.25, 1.75),
        "query_time": draw_query_time(jax.random.fold_in(key_list[12], 71), 0),
        "key_time": draw_key_time(jax.random.fold_in(key_list[12], 71), 0),
        "value_time": bell_draw(key_list[4], (WIDTH, WIDTH), WIDTH ** -0.5, 0.375),
        "output_time": bell_draw(key_list[5], (WIDTH, WIDTH), WIDTH ** -0.5, 0.375),
        "gain_space": jnp.clip(1.0 + 0.15 * jax.random.normal(key_list[6], (WIDTH,), jnp.float32), 0.25, 1.75),
        "query_space": draw_query_space(jax.random.fold_in(key_list[12], 71), 0),
        "key_space": draw_key_space(jax.random.fold_in(key_list[12], 71), 0),
        "value_space": bell_draw(key_list[9], (WIDTH, WIDTH), WIDTH ** -0.5, 0.375),
        "output_space": bell_draw(key_list[10], (WIDTH, WIDTH), WIDTH ** -0.5, 0.375),
        "neighbours": draw_neighbours(jax.random.fold_in(key_list[12], 71), 0),
    }


EPS = 1e-05
ROT_PERIOD = 1024

def rms_scale(rows, gain):
    values = rows.astype(jnp.float32)
    square_mean = lax.optimization_barrier(jnp.mean(values * values, axis=-1, keepdims=True))
    return (values * lax.rsqrt(square_mean + EPS) * gain).astype(jnp.bfloat16)

def project_rows(rows, weight):
    flat = rows.reshape(-1, rows.shape[-1])
    result = jnp.dot(flat, weight, preferred_element_type=jnp.float32)
    return result.reshape(rows.shape[:-1] + (weight.shape[1],))

def rotate_pairs(values, positions, heads):
    features = values.shape[-1]
    head_dim = features // heads
    half = head_dim // 2
    freqs = jnp.power(10000.0, -jnp.arange(half, dtype=jnp.float32) / half)
    angle = (positions % ROT_PERIOD).astype(jnp.float32)[:, None] * freqs[None, :]
    cosine = jnp.cos(angle)[:, None, :]
    sine = jnp.sin(angle)[:, None, :]
    shaped = values.reshape(values.shape[:-1] + (heads, head_dim))
    first = shaped[..., :half]
    second = shaped[..., half:]
    turned = jnp.concatenate([first * cosine - second * sine, first * sine + second * cosine], axis=-1)
    return turned.reshape(values.shape)

def temporal_attend(normed, query_time, key_time, value_time):
    frames, count, features = normed.shape
    head_dim = features // HEADS
    t_query = project_rows(normed, query_time).astype(jnp.bfloat16).reshape(frames, count, HEADS, head_dim)
    t_key = project_rows(normed, key_time).astype(jnp.bfloat16).reshape(frames, count, HEADS, head_dim)
    t_value = project_rows(normed, value_time).astype(jnp.bfloat16).reshape(frames, count, HEADS, head_dim)
    scores = jnp.einsum('fghd,eghd->ghfe', t_query.astype(jnp.float32), t_key.astype(jnp.float32)) / jnp.sqrt(jnp.float32(head_dim))
    weights = jax.nn.softmax(scores, axis=-1).astype(jnp.bfloat16)
    result = jnp.einsum('ghfe,eghd->fghd', weights.astype(jnp.float32), t_value.astype(jnp.float32))
    return result.astype(jnp.bfloat16).reshape(frames, count, features)

def reference(state_tokens, gain_time, query_time, key_time, value_time, output_time, gain_space, query_space, key_space, value_space, output_space, neighbours):
    head_dim = WIDTH // HEADS
    groups = TOKENS // TOK_DEV

    def temporal_group(group_index):
        shard_rows = lax.dynamic_slice_in_dim(state_tokens, group_index * TOK_DEV, TOK_DEV, 1)
        normed = rms_scale(shard_rows, gain_time)
        attended = temporal_attend(normed, query_time, key_time, value_time)
        return (shard_rows.astype(jnp.float32) + project_rows(attended, output_time)).astype(jnp.bfloat16)
    middle = lax.map(temporal_group, jnp.arange(groups, dtype=jnp.int32))
    middle = jnp.moveaxis(middle, 0, 1).reshape(FRAMES, TOKENS, WIDTH)
    normed_space = rms_scale(middle, gain_space)
    positions = jnp.arange(TOKENS, dtype=jnp.int32)
    space_query = rotate_pairs(project_rows(normed_space, query_space), positions, HEADS).astype(jnp.bfloat16)
    space_key = rotate_pairs(project_rows(normed_space, key_space), positions, HEADS).astype(jnp.bfloat16)
    space_value = project_rows(normed_space, value_space).astype(jnp.bfloat16)
    query_blocks = space_query.reshape(FRAMES, BLOCKS, BLOCK, WIDTH)
    key_blocks = space_key.reshape(FRAMES, BLOCKS, BLOCK, WIDTH)
    value_blocks = space_value.reshape(FRAMES, BLOCKS, BLOCK, WIDTH)

    def spatial_block(block_index):
        block_ids = neighbours[block_index]
        valid_slot = block_ids >= 0
        safe_ids = jnp.where(valid_slot, block_ids, 0)
        gathered_keys = key_blocks[:, safe_ids].reshape(FRAMES, NEIGHBOUR_COUNT * BLOCK, HEADS, head_dim)
        gathered_values = value_blocks[:, safe_ids].reshape(FRAMES, NEIGHBOUR_COUNT * BLOCK, HEADS, head_dim)
        key_mask = jnp.repeat(valid_slot, BLOCK)
        query = query_blocks[:, block_index].reshape(FRAMES, BLOCK, HEADS, head_dim)
        scores = jnp.einsum('frhd,fkhd->fhrk', query.astype(jnp.float32), gathered_keys.astype(jnp.float32)) / jnp.sqrt(jnp.float32(head_dim))
        scores = jnp.where(key_mask[None, None, None, :], scores, -1e+30)
        weights = jax.nn.softmax(scores, axis=-1).astype(jnp.bfloat16)
        result = jnp.einsum('fhrk,fkhd->frhd', weights.astype(jnp.float32), gathered_values.astype(jnp.float32))
        return result.astype(jnp.bfloat16).reshape(FRAMES, BLOCK, WIDTH)
    attended = lax.map(spatial_block, jnp.arange(BLOCKS, dtype=jnp.int32))
    attended = jnp.moveaxis(attended, 0, 1).reshape(FRAMES, TOKENS, WIDTH)
    return (middle.astype(jnp.float32) + project_rows(attended, output_space)).astype(jnp.bfloat16)
```

```python
import functools
import math

import jax
import jax.numpy as jnp
import numpy as np
from jax import lax
from jax.experimental import pallas as pl
from jax.experimental.pallas import tpu as pltpu
from jax.sharding import PartitionSpec as P

HEADS = 8
BLOCK = 128
NEIGHBOUR_COUNT = 9
EPS = 1e-05
ROT_PERIOD = 1024
NEG = -1e30
F32 = jnp.float32
BF16 = jnp.bfloat16
MESH = pl.DeviceIdType.MESH


def nt(a, b):
    return lax.dot_general(a, b, (((1,), (1,)), ((), ())), preferred_element_type=F32)


def nn(a, b):
    return lax.dot_general(a, b, (((1,), (0,)), ((), ())), preferred_element_type=F32)


def rms(values, gain):
    square_mean = jnp.mean(values * values, axis=-1, keepdims=True)
    return values * lax.rsqrt(square_mean + EPS) * gain


def head_pair(rows, pair, head_dim):
    lane_head = lax.broadcasted_iota(jnp.int32, rows.shape, 1) // head_dim
    zero = jnp.zeros_like(rows)
    return jnp.concatenate(
        [jnp.where(lane_head == 2 * pair + k, rows, zero) for k in range(2)], axis=0
    )


def pair_result(total, head_dim, count):
    inverse = 1.0 / total[2 * head_dim : 2 * head_dim + 1, :]
    scaled = total[: 2 * head_dim, :] * inverse
    return jnp.concatenate(
        [scaled[:head_dim, :count], scaled[head_dim:, count:]], axis=0
    )


def time_kernel(x_ref, gain_ref, wq_ref, wk_ref, wv_ref, out_ref, norm_ref, att_ref):
    frames, tokens, width = x_ref.shape
    head_dim = width // HEADS
    scale = math.log2(math.e) / math.sqrt(head_dim)
    step = BLOCK // frames
    gain = gain_ref[...]

    def norm_frame(f, carry):
        norm_ref[f] = rms(x_ref[f].astype(F32), gain)
        return carry

    lax.fori_loop(0, frames, norm_frame, 0)
    wv_t = wv_ref[...].astype(F32).T.astype(BF16)
    row = lax.broadcasted_iota(jnp.int32, (BLOCK, 2 * BLOCK), 0)
    column = lax.broadcasted_iota(jnp.int32, (BLOCK, 2 * BLOCK), 1)
    same = (row % step) == (column % step)
    ones = jnp.ones((16, BLOCK), BF16)

    def chunk(i, carry):
        at = pl.ds(pl.multiple_of(i * step, step), step)
        rows = norm_ref[:, at, :].reshape(BLOCK, width).astype(BF16)
        query = (nn(rows, wq_ref[...]) * scale).astype(BF16)
        key = nn(rows, wk_ref[...]).astype(BF16)
        value_t = nt(wv_t, rows).astype(BF16)
        parts = []
        for pair in range(HEADS // 2):
            scores = nt(key, head_pair(query, pair, head_dim))
            scores = jnp.where(same, scores, NEG)
            top = jnp.max(scores, axis=0, keepdims=True)
            weights = jnp.exp2(scores - top).astype(BF16)
            low = 2 * pair * head_dim
            held = jnp.concatenate([value_t[low : low + 2 * head_dim], ones], axis=0)
            parts.append(pair_result(nn(held, weights), head_dim, BLOCK))
        att_ref[:, at, :] = jnp.concatenate(parts, axis=0).T.reshape(frames, step, width)
        return carry

    lax.fori_loop(0, tokens // step, chunk, 0)

    def round_frame(f, carry):
        out_ref[f] = att_ref[f].astype(BF16)
        return carry

    lax.fori_loop(0, frames, round_frame, 0)


def time_attend(rows, gain, wq, wk, wv):
    frames, tokens, width = rows.shape
    vmem = pl.BlockSpec(memory_space=pltpu.VMEM)
    return pl.pallas_call(
        time_kernel,
        out_shape=jax.ShapeDtypeStruct(rows.shape, BF16),
        in_specs=[vmem] * 5,
        out_specs=vmem,
        scratch_shapes=[
            pltpu.VMEM(rows.shape, F32),
            pltpu.VMEM(rows.shape, F32),
        ],
        compiler_params=pltpu.CompilerParams(vmem_limit_bytes=32 << 20),
    )(rows, gain.reshape(1, width), wq, wk, wv)


def swapped(weight):
    wide = weight.astype(F32)
    width = wide.shape[1]
    half = width // HEADS // 2
    lane = lax.broadcasted_iota(jnp.int32, wide.shape, 1)
    ahead = pltpu.roll(wide, width - half, 1)
    behind = pltpu.roll(wide, half, 1)
    return jnp.where(lane % (2 * half) < half, -ahead, behind).astype(BF16)


def space_kernel(
    nbr_ref,
    state_ref,
    ret_ref,
    wt_ref,
    gain_ref,
    wq_ref,
    wk_ref,
    wv_ref,
    wo_ref,
    cos_ref,
    sin_ref,
    out_ref,
    norm_ref,
    mid_ref,
    q_ref,
    k_ref,
    v_ref,
    wqs_ref,
    wks_ref,
    wvt_ref,
    kc_ref,
    s_ref,
    att_ref,
    send_l,
    recv_l,
    send_r,
    recv_r,
):
    blocks = mid_ref.shape[0]
    width = state_ref.shape[-1]
    head_dim = width // HEADS
    scale = math.log2(math.e) / math.sqrt(head_dim)
    tile = lax.axis_index("tile")
    tiles = lax.axis_size("tile")
    left = lax.rem(tile + tiles - 1, tiles)
    right = lax.rem(tile + 1, tiles)
    barrier = pltpu.get_barrier_semaphore()
    for peer in (left, right):
        pl.semaphore_signal(barrier, inc=1, device_id={"tile": peer}, device_id_type=MESH)

    def to_left(j):
        return pltpu.make_async_remote_copy(
            src_ref=norm_ref.at[blocks + j],
            dst_ref=norm_ref.at[2 * blocks + j],
            send_sem=send_l.at[j],
            recv_sem=recv_l.at[j],
            device_id={"tile": left},
            device_id_type=MESH,
        )

    def to_right(j):
        return pltpu.make_async_remote_copy(
            src_ref=norm_ref.at[blocks + j],
            dst_ref=norm_ref.at[j],
            send_sem=send_r.at[j],
            recv_sem=recv_r.at[j],
            device_id={"tile": right},
            device_id_type=MESH,
        )

    gain = gain_ref[...]

    def middle(j, carry):
        at = pl.ds(pl.multiple_of(j * BLOCK, BLOCK), BLOCK)
        mid = (state_ref[at, :].astype(F32) + nn(ret_ref[at, :], wt_ref[...])).astype(BF16)
        mid_ref[j] = mid
        norm_ref[blocks + j] = rms(mid.astype(F32), gain).astype(BF16)
        return carry

    lax.fori_loop(0, blocks, middle, 0)
    pl.semaphore_wait(barrier, 2)

    def send(j, carry):
        to_left(j).start()
        to_right(blocks - 1 - j).start()
        return carry

    lax.fori_loop(0, blocks, send, 0)

    wqs_ref[...] = swapped(wq_ref[...])
    wks_ref[...] = swapped(wk_ref[...])
    wvt_ref[...] = wv_ref[...].astype(F32).T.astype(BF16)

    def turn(rows, weight_ref, swap_ref, j):
        at = pl.ds(pl.multiple_of(j * BLOCK, BLOCK), BLOCK)
        cosine = jnp.concatenate([cos_ref[at, :]] * 2, axis=1)
        sine = jnp.concatenate([sin_ref[at, :]] * 2, axis=1)
        return nn(rows, weight_ref[...]) * cosine + nn(rows, swap_ref[...]) * sine

    ones = jnp.ones((16, BLOCK), BF16)

    def key_value(g, j):
        rows = norm_ref[g]
        k_ref[g] = turn(rows, wk_ref, wks_ref, j).astype(BF16)
        value_t = nt(wvt_ref[...], rows).astype(BF16)
        for pair in range(HEADS // 2):
            low = 2 * pair * head_dim
            v_ref[g, pair] = jnp.concatenate(
                [value_t[low : low + 2 * head_dim], ones], axis=0
            )

    def own(j, carry):
        q_ref[j] = (turn(norm_ref[blocks + j], wq_ref, wqs_ref, j) * scale).astype(BF16)
        key_value(blocks + j, j)
        return carry

    lax.fori_loop(0, blocks, own, 0)

    first = (tile - 1) * blocks
    total_blocks = tiles * blocks

    def place(b, m):
        entry = nbr_ref[b, m]
        offset = entry - first
        offset = jnp.where(offset < 0, offset + total_blocks, offset)
        offset = jnp.where(offset >= total_blocks, offset - total_blocks, offset)
        offset = jnp.minimum(offset, 3 * blocks - 1)
        return jnp.where(entry < 0, blocks + b, offset)

    last_rows = (NEIGHBOUR_COUNT - 1) * BLOCK

    def attend(b):
        places = [place(b, m) for m in range(NEIGHBOUR_COUNT)]
        bias = jnp.where(nbr_ref[b, NEIGHBOUR_COUNT - 1] < 0, NEG, 0.0).astype(F32)
        for m in range(NEIGHBOUR_COUNT):
            kc_ref[m * BLOCK : (m + 1) * BLOCK, :] = k_ref[places[m]]
        query = q_ref[b]
        for pair in range(HEADS // 2):
            slot = pair % 2
            scores = nt(kc_ref[...], head_pair(query, pair, head_dim))
            s_ref[slot] = scores
            tail = s_ref[slot, last_rows:, :] + bias
            top = jnp.maximum(
                jnp.max(scores[:last_rows], axis=0, keepdims=True),
                jnp.max(tail, axis=0, keepdims=True),
            )
            weights = jnp.concatenate(
                [
                    jnp.exp2(s_ref[slot, :last_rows, :] - top).astype(BF16),
                    jnp.exp2(tail - top).astype(BF16),
                ],
                axis=0,
            )
            held = jnp.concatenate([v_ref[g, pair] for g in places], axis=1)
            low = 2 * pair * head_dim
            att_ref[low : low + 2 * head_dim, :] = pair_result(
                nn(held, weights), head_dim, BLOCK
            )
        attended = att_ref[...].T.astype(BF16)
        at = pl.ds(pl.multiple_of(b * BLOCK, BLOCK), BLOCK)
        out_ref[at, :] = (mid_ref[b].astype(F32) + nn(attended, wo_ref[...])).astype(BF16)

    def arrive(j, carry):
        to_left(j).wait_recv()
        key_value(2 * blocks + j, j)
        to_right(blocks - 1 - j).wait_recv()
        key_value(blocks - 1 - j, blocks - 1 - j)
        return carry

    half = blocks // 2
    lax.fori_loop(0, half + 1, arrive, 0)

    def attend_pair(i, carry):
        attend(half - 1 - i)
        lax.fori_loop(half + 1 + i, jnp.minimum(half + 2 + i, blocks), arrive, 0)
        attend(half + i)
        return carry

    lax.fori_loop(0, half, attend_pair, 0)

    def sent(j, carry):
        to_left(j).wait_send()
        to_right(blocks - 1 - j).wait_send()
        return carry

    lax.fori_loop(0, blocks, sent, 0)


def rotary_tables(tokens, head_dim):
    half = head_dim // 2
    freqs = np.power(np.float32(10000.0), -np.arange(half, dtype=np.float32) / np.float32(half))
    angle = np.arange(tokens, dtype=np.float32)[:, None] * freqs[None, :].astype(np.float32)
    angle = np.tile(angle.astype(np.float64), (1, BLOCK // half))
    return np.cos(angle).astype(np.float32), np.sin(angle).astype(np.float32)


def space_attend(neighbours, state, returned, wt, gain, wq, wk, wv, wo):
    tokens, width = state.shape
    blocks = tokens // BLOCK
    head_dim = width // HEADS
    cosine, sine = rotary_tables(tokens, head_dim)
    vmem = pl.BlockSpec(memory_space=pltpu.VMEM)
    return pl.pallas_call(
        space_kernel,
        out_shape=jax.ShapeDtypeStruct(state.shape, BF16),
        in_specs=[pl.BlockSpec(memory_space=pltpu.SMEM)] + [vmem] * 10,
        out_specs=vmem,
        scratch_shapes=[
            pltpu.VMEM((3 * blocks, BLOCK, width), BF16),
            pltpu.VMEM((blocks, BLOCK, width), BF16),
            pltpu.VMEM((blocks, BLOCK, width), BF16),
            pltpu.VMEM((3 * blocks, BLOCK, width), BF16),
            pltpu.VMEM((3 * blocks, HEADS // 2, 2 * head_dim + 16, BLOCK), BF16),
            pltpu.VMEM((width, width), BF16),
            pltpu.VMEM((width, width), BF16),
            pltpu.VMEM((width, width), BF16),
            pltpu.VMEM((NEIGHBOUR_COUNT * BLOCK, width), BF16),
            pltpu.VMEM((2, NEIGHBOUR_COUNT * BLOCK, 2 * BLOCK), F32),
            pltpu.VMEM((width, BLOCK), F32),
            pltpu.SemaphoreType.DMA((blocks,)),
            pltpu.SemaphoreType.DMA((blocks,)),
            pltpu.SemaphoreType.DMA((blocks,)),
            pltpu.SemaphoreType.DMA((blocks,)),
        ],
        compiler_params=pltpu.CompilerParams(
            vmem_limit_bytes=48 << 20, collective_id=1, has_side_effects=True
        ),
    )(
        neighbours,
        state,
        returned,
        wt,
        gain.reshape(1, width),
        wq,
        wk,
        wv,
        wo,
        jnp.asarray(cosine),
        jnp.asarray(sine),
    )


def body(
    state_tokens,
    gain_time,
    query_time,
    key_time,
    value_time,
    output_time,
    gain_space,
    query_space,
    key_space,
    value_space,
    output_space,
    neighbours,
):
    frames_here, tokens_here, features = state_tokens.shape
    frame_count = lax.axis_size("frame")
    part = tokens_here // frame_count
    split_rows = state_tokens.reshape(frames_here, frame_count, part, features)
    shard_rows = lax.all_to_all(split_rows, "frame", split_axis=1, concat_axis=0, tiled=True)
    attended = time_attend(
        shard_rows.reshape(frame_count, part, features), gain_time, query_time, key_time, value_time
    )
    returned = lax.all_to_all(
        attended.reshape(frame_count, 1, part, features),
        "frame",
        split_axis=0,
        concat_axis=1,
        tiled=True,
    )
    updated = space_attend(
        neighbours,
        state_tokens.reshape(tokens_here, features),
        returned.reshape(tokens_here, features),
        output_time,
        gain_space,
        query_space,
        key_space,
        value_space,
        output_space,
    )
    return updated.reshape(state_tokens.shape)


def solution(mesh):
    return jax.shard_map(
        body,
        mesh=mesh,
        in_specs=(P("frame", "tile", None),) + (P(),) * 10 + (P("tile", None),),
        out_specs=P("frame", "tile", None),
        check_vma=False,
    )
```

```python
import functools
import math

import jax
import jax.numpy as jnp
import numpy as np
from jax import lax
from jax.experimental import pallas as pl
from jax.experimental.pallas import tpu as pltpu
from jax.sharding import PartitionSpec as P

HEADS = 8
BLOCK = 128
NEIGHBOUR_COUNT = 9
EPS = 1e-05
ROT_PERIOD = 1024
NEG = -1e30
F32 = jnp.float32
BF16 = jnp.bfloat16
MESH = pl.DeviceIdType.MESH


def nt(a, b):
    return lax.dot_general(a, b, (((1,), (1,)), ((), ())), preferred_element_type=F32)


def nn(a, b):
    return lax.dot_general(a, b, (((1,), (0,)), ((), ())), preferred_element_type=F32)


def rms(values, gain):
    square_mean = jnp.mean(values * values, axis=-1, keepdims=True)
    return values * lax.rsqrt(square_mean + EPS) * gain


def head_pair(rows, pair, head_dim):
    lane_head = lax.broadcasted_iota(jnp.int32, rows.shape, 1) // head_dim
    zero = jnp.zeros_like(rows)
    return jnp.concatenate(
        [jnp.where(lane_head == 2 * pair + k, rows, zero) for k in range(2)], axis=0
    )


def pair_result(total, head_dim, count):
    inverse = 1.0 / total[2 * head_dim : 2 * head_dim + 1, :]
    scaled = total[: 2 * head_dim, :] * inverse
    return jnp.concatenate(
        [scaled[:head_dim, :count], scaled[head_dim:, count:]], axis=0
    )


def time_kernel(
    x_ref, gain_ref, wq_ref, wk_ref, wv_ref, out_ref, q_ref, k_ref, v_ref
):
    frames, tokens, width = x_ref.shape
    head_dim = width // HEADS
    scale = math.log2(math.e) / math.sqrt(head_dim)
    step = BLOCK // frames
    gain = gain_ref[...]
    wv_t = wv_ref[...].astype(F32).T.astype(BF16)

    def at(i):
        return pl.ds(pl.multiple_of(i * 2 * step, 2 * step), 2 * step)

    def project(i, carry):
        normed = rms(x_ref[:, at(i), :].astype(F32), gain)
        rows = jnp.concatenate(
            [
                normed[:, k * step : (k + 1) * step].reshape(BLOCK, width).astype(BF16)
                for k in range(2)
            ],
            axis=0,
        )
        query = (nn(rows, wq_ref[...]) * scale).astype(BF16)
        key = nn(rows, wk_ref[...]).astype(BF16)
        value_t = nt(wv_t, rows).astype(BF16)
        q_ref[pl.ds(2 * i, 2)] = query.reshape(2, BLOCK, width)
        k_ref[pl.ds(2 * i, 2)] = key.reshape(2, BLOCK, width)
        for k in range(2):
            v_ref[2 * i + k] = value_t[:, k * BLOCK : (k + 1) * BLOCK]
        return carry

    pairs = tokens // step // 2
    lax.fori_loop(0, pairs, project, 0)

    row = lax.broadcasted_iota(jnp.int32, (BLOCK, 2 * BLOCK), 0)
    column = lax.broadcasted_iota(jnp.int32, (BLOCK, 2 * BLOCK), 1)
    same = (row % step) == (column % step)
    ones = jnp.ones((16, BLOCK), BF16)

    def attend(i, carry):
        halves = []
        units = [(k, pair) for k in range(2) for pair in range(HEADS // 2)]
        scores = {
            (k, pair): jnp.where(
                same, nt(k_ref[2 * i + k], head_pair(q_ref[2 * i + k], pair, head_dim)), NEG
            )
            for k, pair in units
        }
        weights = {
            unit: jnp.exp2(value - jnp.max(value, axis=0, keepdims=True)).astype(BF16)
            for unit, value in scores.items()
        }
        for k in range(2):
            value_t = v_ref[2 * i + k]
            parts = []
            for pair in range(HEADS // 2):
                low = 2 * pair * head_dim
                held = jnp.concatenate([value_t[low : low + 2 * head_dim], ones], axis=0)
                parts.append(pair_result(nn(held, weights[k, pair]), head_dim, BLOCK))
            halves.append(jnp.concatenate(parts, axis=0).T.reshape(frames, step, width))
        out_ref[:, at(i), :] = jnp.concatenate(halves, axis=1).astype(BF16)
        return carry

    lax.fori_loop(0, pairs, attend, 0)


def time_attend(rows, gain, wq, wk, wv):
    frames, tokens, width = rows.shape
    chunks = frames * tokens // BLOCK
    vmem = pl.BlockSpec(memory_space=pltpu.VMEM)
    return pl.pallas_call(
        time_kernel,
        out_shape=jax.ShapeDtypeStruct(rows.shape, BF16),
        in_specs=[vmem] * 5,
        out_specs=vmem,
        scratch_shapes=[
            pltpu.VMEM((chunks, BLOCK, width), BF16),
            pltpu.VMEM((chunks, BLOCK, width), BF16),
            pltpu.VMEM((chunks, width, BLOCK), BF16),
        ],
        compiler_params=pltpu.CompilerParams(vmem_limit_bytes=32 << 20),
    )(rows, gain.reshape(1, width), wq, wk, wv)


def swapped(weight):
    wide = weight.astype(F32)
    width = wide.shape[1]
    half = width // HEADS // 2
    lane = lax.broadcasted_iota(jnp.int32, wide.shape, 1)
    ahead = pltpu.roll(wide, width - half, 1)
    behind = pltpu.roll(wide, half, 1)
    return jnp.where(lane % (2 * half) < half, -ahead, behind).astype(BF16)


def space_kernel(
    nbr_ref,
    state_ref,
    ret_ref,
    wt_ref,
    gain_ref,
    wq_ref,
    wk_ref,
    wv_ref,
    wo_ref,
    cos_ref,
    sin_ref,
    out_ref,
    norm_ref,
    mid_ref,
    q_ref,
    k_ref,
    v_ref,
    wq2_ref,
    wk2_ref,
    wvt_ref,
    kca_ref,
    kcb_ref,
    s_ref,
    att_ref,
    send_l,
    recv_l,
    send_r,
    recv_r,
):
    blocks = mid_ref.shape[0]
    width = state_ref.shape[-1]
    head_dim = width // HEADS
    scale = math.log2(math.e) / math.sqrt(head_dim)
    tile = lax.axis_index("tile")
    tiles = lax.axis_size("tile")
    left = lax.rem(tile + tiles - 1, tiles)
    right = lax.rem(tile + 1, tiles)
    barrier = pltpu.get_barrier_semaphore()
    for peer in (left, right):
        pl.semaphore_signal(barrier, inc=1, device_id={"tile": peer}, device_id_type=MESH)

    def to_left(j):
        return pltpu.make_async_remote_copy(
            src_ref=norm_ref.at[blocks + j],
            dst_ref=norm_ref.at[2 * blocks + j],
            send_sem=send_l.at[j],
            recv_sem=recv_l.at[j],
            device_id={"tile": left},
            device_id_type=MESH,
        )

    def to_right(j):
        return pltpu.make_async_remote_copy(
            src_ref=norm_ref.at[blocks + j],
            dst_ref=norm_ref.at[j],
            send_sem=send_r.at[j],
            recv_sem=recv_r.at[j],
            device_id={"tile": right},
            device_id_type=MESH,
        )

    gain = gain_ref[...]

    def middle(j, carry):
        at = pl.ds(pl.multiple_of(j * BLOCK, BLOCK), BLOCK)
        mid = (state_ref[at, :].astype(F32) + nn(ret_ref[at, :], wt_ref[...])).astype(BF16)
        mid_ref[j] = mid
        norm_ref[blocks + j] = rms(mid.astype(F32), gain).astype(BF16)
        return carry

    lax.fori_loop(0, blocks, middle, 0)
    pl.semaphore_wait(barrier, 2)

    def send(j, carry):
        to_left(j).start()
        to_right(blocks - 1 - j).start()
        return carry

    lax.fori_loop(0, blocks, send, 0)

    wq2_ref[:, :width] = wq_ref[...]
    wq2_ref[:, width:] = swapped(wq_ref[...])
    wk2_ref[:, :width] = wk_ref[...]
    wk2_ref[:, width:] = swapped(wk_ref[...])
    wvt_ref[...] = wv_ref[...].astype(F32).T.astype(BF16)

    def turn(rows, weight_ref, j):
        at = pl.ds(pl.multiple_of(j * BLOCK, BLOCK), 2 * BLOCK)
        cosine = jnp.concatenate([cos_ref[at, :]] * 2, axis=1)
        sine = jnp.concatenate([sin_ref[at, :]] * 2, axis=1)
        both = nn(rows, weight_ref[...])
        return both[:, :width] * cosine + both[:, width:] * sine

    ones = jnp.ones((16, BLOCK), BF16)

    def key_value(g, j):
        rows = norm_ref[pl.ds(g, 2)].reshape(2 * BLOCK, width)
        k_ref[pl.ds(g, 2)] = turn(rows, wk2_ref, j).astype(BF16).reshape(2, BLOCK, width)
        value_t = nt(wvt_ref[...], rows).astype(BF16)
        for pair in range(HEADS // 2):
            low = 2 * pair * head_dim
            for k in range(2):
                v_ref[g + k, pair] = jnp.concatenate(
                    [value_t[low : low + 2 * head_dim, k * BLOCK : (k + 1) * BLOCK], ones], axis=0
                )

    def own(i, carry):
        j = 2 * i
        rows = norm_ref[pl.ds(blocks + j, 2)].reshape(2 * BLOCK, width)
        query = (turn(rows, wq2_ref, j) * scale).astype(BF16)
        q_ref[pl.ds(j, 2)] = query.reshape(2, BLOCK, width)
        key_value(blocks + j, j)
        return carry

    lax.fori_loop(0, blocks // 2, own, 0)

    first = (tile - 1) * blocks
    total_blocks = tiles * blocks

    def place(b, m):
        entry = nbr_ref[b, m]
        offset = entry - first
        offset = jnp.where(offset < 0, offset + total_blocks, offset)
        offset = jnp.where(offset >= total_blocks, offset - total_blocks, offset)
        offset = jnp.minimum(offset, 3 * blocks - 1)
        return jnp.where(entry < 0, blocks + b, offset)

    def places(b):
        return [place(b, m) for m in range(NEIGHBOUR_COUNT)]

    last_rows = (NEIGHBOUR_COUNT - 1) * BLOCK

    def bias_of(b):
        return jnp.where(nbr_ref[b, NEIGHBOUR_COUNT - 1] < 0, NEG, 0.0).astype(F32)

    def fill(kc_ref, at):
        for m in range(NEIGHBOUR_COUNT):
            kc_ref[m * BLOCK : (m + 1) * BLOCK, :] = k_ref[at[m]]

    def score(kc_ref, query, pair, bias):
        scores = nt(kc_ref[...], head_pair(query, pair, head_dim))
        tail = scores[last_rows:] + bias
        s_ref[pair, :last_rows, :] = scores[:last_rows]
        s_ref[pair, last_rows:, :] = tail
        return jnp.maximum(
            jnp.max(scores[:last_rows], axis=0, keepdims=True),
            jnp.max(tail, axis=0, keepdims=True),
        )

    def weigh(at, pair, top):
        weights = jnp.exp2(s_ref[pair] - top).astype(BF16)
        held = jnp.concatenate([v_ref[g, pair] for g in at], axis=1)
        low = 2 * pair * head_dim
        att_ref[low : low + 2 * head_dim, :] = pair_result(nn(held, weights), head_dim, BLOCK)

    def arrive(i, carry):
        j = 2 * i
        for k in range(2):
            to_left(j + k).wait_recv()
            to_right(blocks - 1 - j - k).wait_recv()
        key_value(2 * blocks + j, j)
        key_value(blocks - 2 - j, blocks - 2 - j)
        return carry

    lax.fori_loop(0, blocks // 2, arrive, 0)

    def attend(b, tops):
        here = places(b)
        after = jnp.minimum(b + 1, blocks - 1)
        there = places(after)
        query = q_ref[b]
        bias = bias_of(b)
        fill(kca_ref, there)
        query_after = q_ref[after]
        bias_after = bias_of(after)
        late = [score(kcb_ref, query, 2, bias)]
        weigh(here, 0, tops[0])
        late.append(score(kcb_ref, query, 3, bias))
        weigh(here, 1, tops[1])
        fill(kcb_ref, there)
        early = [score(kca_ref, query_after, 0, bias_after)]
        weigh(here, 2, late[0])
        early.append(score(kca_ref, query_after, 1, bias_after))
        weigh(here, 3, late[1])
        early = tuple(early)
        attended = att_ref[...].T.astype(BF16)
        at = pl.ds(pl.multiple_of(b * BLOCK, BLOCK), BLOCK)
        out_ref[at, :] = (mid_ref[b].astype(F32) + nn(attended, wo_ref[...])).astype(BF16)
        return early

    at_first = places(0)
    fill(kca_ref, at_first)
    fill(kcb_ref, at_first)
    query_first = q_ref[0]
    bias_first = bias_of(0)
    lax.fori_loop(
        0,
        blocks,
        attend,
        tuple(score(kca_ref, query_first, pair, bias_first) for pair in (0, 1)),
    )

    def sent(j, carry):
        to_left(j).wait_send()
        to_right(blocks - 1 - j).wait_send()
        return carry

    lax.fori_loop(0, blocks, sent, 0)


def rotary_tables(tokens, head_dim):
    half = head_dim // 2
    freqs = np.power(np.float32(10000.0), -np.arange(half, dtype=np.float32) / np.float32(half))
    angle = np.arange(tokens, dtype=np.float32)[:, None] * freqs[None, :].astype(np.float32)
    angle = np.tile(angle.astype(np.float64), (1, BLOCK // half))
    return np.cos(angle).astype(np.float32), np.sin(angle).astype(np.float32)


def space_attend(neighbours, state, returned, wt, gain, wq, wk, wv, wo):
    tokens, width = state.shape
    blocks = tokens // BLOCK
    head_dim = width // HEADS
    cosine, sine = rotary_tables(tokens, head_dim)
    vmem = pl.BlockSpec(memory_space=pltpu.VMEM)
    return pl.pallas_call(
        space_kernel,
        out_shape=jax.ShapeDtypeStruct(state.shape, BF16),
        in_specs=[pl.BlockSpec(memory_space=pltpu.SMEM)] + [vmem] * 10,
        out_specs=vmem,
        scratch_shapes=[
            pltpu.VMEM((3 * blocks, BLOCK, width), BF16),
            pltpu.VMEM((blocks, BLOCK, width), BF16),
            pltpu.VMEM((blocks, BLOCK, width), BF16),
            pltpu.VMEM((3 * blocks, BLOCK, width), BF16),
            pltpu.VMEM((3 * blocks, HEADS // 2, 2 * head_dim + 16, BLOCK), BF16),
            pltpu.VMEM((width, 2 * width), BF16),
            pltpu.VMEM((width, 2 * width), BF16),
            pltpu.VMEM((width, width), BF16),
            pltpu.VMEM((NEIGHBOUR_COUNT * BLOCK, width), BF16),
            pltpu.VMEM((NEIGHBOUR_COUNT * BLOCK, width), BF16),
            pltpu.VMEM((HEADS // 2, NEIGHBOUR_COUNT * BLOCK, 2 * BLOCK), F32),
            pltpu.VMEM((width, BLOCK), F32),
            pltpu.SemaphoreType.DMA((blocks,)),
            pltpu.SemaphoreType.DMA((blocks,)),
            pltpu.SemaphoreType.DMA((blocks,)),
            pltpu.SemaphoreType.DMA((blocks,)),
        ],
        compiler_params=pltpu.CompilerParams(
            vmem_limit_bytes=48 << 20, collective_id=1, has_side_effects=True
        ),
    )(
        neighbours,
        state,
        returned,
        wt,
        gain.reshape(1, width),
        wq,
        wk,
        wv,
        wo,
        jnp.asarray(cosine),
        jnp.asarray(sine),
    )


def body(
    state_tokens,
    gain_time,
    query_time,
    key_time,
    value_time,
    output_time,
    gain_space,
    query_space,
    key_space,
    value_space,
    output_space,
    neighbours,
):
    frames_here, tokens_here, features = state_tokens.shape
    frame_count = lax.axis_size("frame")
    part = tokens_here // frame_count
    split_rows = state_tokens.reshape(frames_here, frame_count, part, features)
    shard_rows = lax.all_to_all(split_rows, "frame", split_axis=1, concat_axis=0, tiled=True)
    attended = time_attend(
        shard_rows.reshape(frame_count, part, features), gain_time, query_time, key_time, value_time
    )
    returned = lax.all_to_all(
        attended.reshape(frame_count, 1, part, features),
        "frame",
        split_axis=0,
        concat_axis=1,
        tiled=True,
    )
    updated = space_attend(
        neighbours,
        state_tokens.reshape(tokens_here, features),
        returned.reshape(tokens_here, features),
        output_time,
        gain_space,
        query_space,
        key_space,
        value_space,
        output_space,
    )
    return updated.reshape(state_tokens.shape)


def solution(mesh):
    return jax.shard_map(
        body,
        mesh=mesh,
        in_specs=(P("frame", "tile", None),) + (P(),) * 10 + (P("tile", None),),
        out_specs=P("frame", "tile", None),
        check_vma=False,
    )
```

```python
import functools
import math

import jax
import jax.numpy as jnp
import numpy as np
from jax import lax
from jax.experimental import pallas as pl
from jax.experimental.pallas import tpu as pltpu
from jax.sharding import PartitionSpec as P

HEADS = 8
BLOCK = 128
NEIGHBOUR_COUNT = 9
EPS = 1e-05
ROT_PERIOD = 1024
NEG = -1e30
F32 = jnp.float32
BF16 = jnp.bfloat16
MESH = pl.DeviceIdType.MESH


def nt(a, b):
    return lax.dot_general(a, b, (((1,), (1,)), ((), ())), preferred_element_type=F32)


def nn(a, b):
    return lax.dot_general(a, b, (((1,), (0,)), ((), ())), preferred_element_type=F32)


def rms(values, gain):
    square_mean = jnp.mean(values * values, axis=-1, keepdims=True)
    return values * lax.rsqrt(square_mean + EPS) * gain


def head_pair(rows, pair, head_dim):
    lane_head = lax.broadcasted_iota(jnp.int32, rows.shape, 1) // head_dim
    zero = jnp.zeros_like(rows)
    return jnp.concatenate(
        [jnp.where(lane_head == 2 * pair + k, rows, zero) for k in range(2)], axis=0
    )


def pair_result(total, head_dim, count):
    inverse = 1.0 / total[2 * head_dim : 2 * head_dim + 1, :]
    scaled = total[: 2 * head_dim, :] * inverse
    return jnp.concatenate(
        [scaled[:head_dim, :count], scaled[head_dim:, count:]], axis=0
    )


def time_chunk(slots, gain, wq, wk, wv_t, same, scale, head_dim):
    frames, tokens, width = slots.shape
    step = tokens // 2
    normed = rms(slots.astype(F32), gain)
    rows = jnp.concatenate(
        [
            normed[:, k * step : (k + 1) * step].reshape(BLOCK, width).astype(BF16)
            for k in range(2)
        ],
        axis=0,
    )
    query = (nn(rows, wq) * scale).astype(BF16)
    key = nn(rows, wk).astype(BF16)
    value_t = nt(wv_t, rows).astype(BF16)
    ones = jnp.ones((16, BLOCK), BF16)
    units = [(k, pair) for k in range(2) for pair in range(HEADS // 2)]
    scores = {}
    for k, pair in units:
        part = slice(k * BLOCK, (k + 1) * BLOCK)
        scores[k, pair] = jnp.where(
            same, nt(key[part], head_pair(query[part], pair, head_dim)), NEG
        )
    weights = {
        unit: jnp.exp2(value - jnp.max(value, axis=0, keepdims=True)).astype(BF16)
        for unit, value in scores.items()
    }
    halves = []
    for k in range(2):
        parts = []
        for pair in range(HEADS // 2):
            low = 2 * pair * head_dim
            held = jnp.concatenate(
                [value_t[low : low + 2 * head_dim, k * BLOCK : (k + 1) * BLOCK], ones], axis=0
            )
            parts.append(pair_result(nn(held, weights[k, pair]), head_dim, BLOCK))
        halves.append(jnp.concatenate(parts, axis=0).T.reshape(frames, step, width))
    return jnp.concatenate(halves, axis=1)


def swapped(weight):
    wide = weight.astype(F32)
    width = wide.shape[1]
    half = width // HEADS // 2
    lane = lax.broadcasted_iota(jnp.int32, wide.shape, 1)
    ahead = pltpu.roll(wide, width - half, 1)
    behind = pltpu.roll(wide, half, 1)
    return jnp.where(lane % (2 * half) < half, -ahead, behind).astype(BF16)


def layer_kernel(
    nbr_ref,
    state_ref,
    gain_t_ref,
    wqt_ref,
    wkt_ref,
    wvt_in_ref,
    wt_ref,
    gain_ref,
    wq_ref,
    wk_ref,
    wv_ref,
    wo_ref,
    cos_ref,
    sin_ref,
    out_ref,
    rows_ref,
    attn_ref,
    ret_ref,
    norm_ref,
    mid_ref,
    q_ref,
    k_ref,
    v_ref,
    wq2_ref,
    wk2_ref,
    wvt_ref,
    wvtt_ref,
    kca_ref,
    kcb_ref,
    s_ref,
    att_ref,
    go_sem,
    come_sem,
    back_sem,
    home_sem,
    send_l,
    recv_l,
    send_r,
    recv_r,
):
    blocks = mid_ref.shape[0]
    width = state_ref.shape[-1]
    head_dim = width // HEADS
    scale = math.log2(math.e) / math.sqrt(head_dim)
    chunks, frames, slab, _ = rows_ref.shape
    half = frames // 2
    per = blocks // chunks
    tile = lax.axis_index("tile")
    tiles = lax.axis_size("tile")
    left = lax.rem(tile + tiles - 1, tiles)
    right = lax.rem(tile + 1, tiles)
    me = lax.axis_index("frame")
    my_side = me // half
    my_place = lax.rem(me, half)

    def peer_at(k):
        return lax.rem(my_side + k // half, 2) * half + lax.rem(my_place + lax.rem(k, half), half)

    def mirror(k):
        return (k // half) * half + lax.rem(half - lax.rem(k, half), half)

    barrier = pltpu.get_barrier_semaphore()

    def greet(k, carry):
        pl.semaphore_signal(
            barrier, inc=1, device_id={"frame": peer_at(k)}, device_id_type=MESH
        )
        return carry

    lax.fori_loop(1, frames, greet, 0)
    for peer in (left, right):
        pl.semaphore_signal(barrier, inc=1, device_id={"tile": peer}, device_id_type=MESH)

    def go(c, k):
        at = pl.ds(pl.multiple_of((c * frames + peer_at(k)) * slab, slab), slab)
        return pltpu.make_async_remote_copy(
            src_ref=state_ref.at[at, :],
            dst_ref=rows_ref.at[c, mirror(k)],
            send_sem=go_sem.at[c],
            recv_sem=come_sem.at[c],
            device_id={"frame": peer_at(k)},
            device_id_type=MESH,
        )

    def back(c, k):
        return pltpu.make_async_remote_copy(
            src_ref=attn_ref.at[c, k],
            dst_ref=ret_ref.at[c, me],
            send_sem=back_sem.at[c],
            recv_sem=home_sem.at[c],
            device_id={"frame": peer_at(k)},
            device_id_type=MESH,
        )

    def whole(ref, c, send_sem, recv_sem):
        return pltpu.make_async_remote_copy(
            src_ref=ref.at[c, pl.ds(0, frames - 1)],
            dst_ref=ref.at[c, pl.ds(0, frames - 1)],
            send_sem=send_sem.at[c],
            recv_sem=recv_sem.at[c],
            device_id={"frame": peer_at(1)},
            device_id_type=MESH,
        )

    def to_left(c):
        return pltpu.make_async_remote_copy(
            src_ref=norm_ref.at[pl.ds(blocks + per * c, per)],
            dst_ref=norm_ref.at[pl.ds(2 * blocks + per * c, per)],
            send_sem=send_l.at[c],
            recv_sem=recv_l.at[c],
            device_id={"tile": left},
            device_id_type=MESH,
        )

    def to_right(c):
        return pltpu.make_async_remote_copy(
            src_ref=norm_ref.at[pl.ds(blocks + per * c, per)],
            dst_ref=norm_ref.at[pl.ds(per * c, per)],
            send_sem=send_r.at[c],
            recv_sem=recv_r.at[c],
            device_id={"tile": right},
            device_id_type=MESH,
        )

    pl.semaphore_wait(barrier, frames + 1)

    def leave(c, carry):
        def one(i, inner):
            go(c, frames - 1 - i).start()
            return inner

        return lax.fori_loop(0, frames - 1, one, carry)

    lax.fori_loop(0, chunks, leave, 0)

    def stay(c, carry):
        at = pl.ds(pl.multiple_of((c * frames + me) * slab, slab), slab)
        rows_ref[c, 0] = state_ref[at, :]
        return carry

    lax.fori_loop(0, chunks, stay, 0)
    wvtt_ref[...] = wvt_in_ref[...].astype(F32).T.astype(BF16)
    wq2_ref[:, :width] = wq_ref[...]
    wq2_ref[:, width:] = swapped(wq_ref[...])
    wk2_ref[:, :width] = wk_ref[...]
    wk2_ref[:, width:] = swapped(wk_ref[...])
    wvt_ref[...] = wv_ref[...].astype(F32).T.astype(BF16)


    row = lax.broadcasted_iota(jnp.int32, (BLOCK, 2 * BLOCK), 0)
    column = lax.broadcasted_iota(jnp.int32, (BLOCK, 2 * BLOCK), 1)
    step = slab // 2
    same = (row % step) == (column % step)

    def over_time(c, carry):
        whole(rows_ref, c, go_sem, come_sem).wait_recv()
        attended = time_chunk(
            rows_ref[c],
            gain_t_ref[...],
            wqt_ref[...],
            wkt_ref[...],
            wvtt_ref[...],
            same,
            scale,
            head_dim,
        )
        attn_ref[c] = attended.astype(BF16)

        def one(i, inner):
            back(c, frames - 1 - i).start()
            return inner

        lax.fori_loop(0, frames - 1, one, 0)
        ret_ref[c, me] = attn_ref[c, 0]
        return carry

    lax.fori_loop(0, chunks, over_time, 0)

    def turn(rows, weight_ref, j):
        at = pl.ds(pl.multiple_of(j * BLOCK, BLOCK), 2 * BLOCK)
        cosine = jnp.concatenate([cos_ref[at, :]] * 2, axis=1)
        sine = jnp.concatenate([sin_ref[at, :]] * 2, axis=1)
        both = nn(rows, weight_ref[...])
        return both[:, :width] * cosine + both[:, width:] * sine

    ones = jnp.ones((16, BLOCK), BF16)

    def key_value(g, j):
        rows = norm_ref[pl.ds(g, 2)].reshape(2 * BLOCK, width)
        k_ref[pl.ds(g, 2)] = turn(rows, wk2_ref, j).astype(BF16).reshape(2, BLOCK, width)
        value_t = nt(wvt_ref[...], rows).astype(BF16)
        for pair in range(HEADS // 2):
            low = 2 * pair * head_dim
            for k in range(2):
                v_ref[g + k, pair] = jnp.concatenate(
                    [value_t[low : low + 2 * head_dim, k * BLOCK : (k + 1) * BLOCK], ones], axis=0
                )

    gain = gain_ref[...]

    def own(c, carry):
        j = per * c
        whole(ret_ref, c, back_sem, home_sem).wait_recv()
        at = pl.ds(pl.multiple_of(c * frames * slab, frames * slab), frames * slab)
        returned = ret_ref[c].reshape(frames * slab, width)
        mid = (state_ref[at, :].astype(F32) + nn(returned, wt_ref[...])).astype(BF16)
        mid_ref[pl.ds(j, per)] = mid.reshape(per, BLOCK, width)
        rows = rms(mid.astype(F32), gain).astype(BF16)
        norm_ref[pl.ds(blocks + j, per)] = rows.reshape(per, BLOCK, width)
        to_left(c).start()
        to_right(c).start()
        query = (turn(rows, wq2_ref, j) * scale).astype(BF16)
        q_ref[pl.ds(j, per)] = query.reshape(per, BLOCK, width)
        key_value(blocks + j, j)
        return carry

    lax.fori_loop(0, chunks, own, 0)

    first = (tile - 1) * blocks
    total_blocks = tiles * blocks

    def place(b, m):
        entry = nbr_ref[b, m]
        offset = entry - first
        offset = jnp.where(offset < 0, offset + total_blocks, offset)
        offset = jnp.where(offset >= total_blocks, offset - total_blocks, offset)
        offset = jnp.minimum(offset, 3 * blocks - 1)
        return jnp.where(entry < 0, blocks + b, offset)

    def places(b):
        return [place(b, m) for m in range(NEIGHBOUR_COUNT)]

    last_rows = (NEIGHBOUR_COUNT - 1) * BLOCK

    def bias_of(b):
        return jnp.where(nbr_ref[b, NEIGHBOUR_COUNT - 1] < 0, NEG, 0.0).astype(F32)

    def fill(kc_ref, at):
        for m in range(NEIGHBOUR_COUNT):
            kc_ref[m * BLOCK : (m + 1) * BLOCK, :] = k_ref[at[m]]

    def score(kc_ref, query, pair, bias):
        scores = nt(kc_ref[...], head_pair(query, pair, head_dim))
        tail = scores[last_rows:] + bias
        s_ref[pair, :last_rows, :] = scores[:last_rows]
        s_ref[pair, last_rows:, :] = tail
        return jnp.maximum(
            jnp.max(scores[:last_rows], axis=0, keepdims=True),
            jnp.max(tail, axis=0, keepdims=True),
        )

    def weigh(at, pair, top):
        weights = jnp.exp2(s_ref[pair] - top).astype(BF16)
        held = jnp.concatenate([v_ref[g, pair] for g in at], axis=1)
        low = 2 * pair * head_dim
        att_ref[low : low + 2 * head_dim, :] = pair_result(nn(held, weights), head_dim, BLOCK)

    def arrive(c, carry):
        to_left(c).wait_recv()
        key_value(2 * blocks + per * c, per * c)
        to_right(c).wait_recv()
        key_value(per * c, per * c)
        return carry

    lax.fori_loop(0, chunks, arrive, 0)

    def attend(b, tops):
        here = places(b)
        after = jnp.minimum(b + 1, blocks - 1)
        there = places(after)
        query = q_ref[b]
        bias = bias_of(b)
        fill(kca_ref, there)
        query_after = q_ref[after]
        bias_after = bias_of(after)
        late = [score(kcb_ref, query, 2, bias)]
        weigh(here, 0, tops[0])
        late.append(score(kcb_ref, query, 3, bias))
        weigh(here, 1, tops[1])
        fill(kcb_ref, there)
        early = [score(kca_ref, query_after, 0, bias_after)]
        weigh(here, 2, late[0])
        early.append(score(kca_ref, query_after, 1, bias_after))
        weigh(here, 3, late[1])
        early = tuple(early)
        attended = att_ref[...].T.astype(BF16)
        at = pl.ds(pl.multiple_of(b * BLOCK, BLOCK), BLOCK)
        out_ref[at, :] = (mid_ref[b].astype(F32) + nn(attended, wo_ref[...])).astype(BF16)
        return early

    at_first = places(0)
    fill(kca_ref, at_first)
    fill(kcb_ref, at_first)
    query_first = q_ref[0]
    bias_first = bias_of(0)
    lax.fori_loop(
        0,
        blocks,
        attend,
        tuple(score(kca_ref, query_first, pair, bias_first) for pair in (0, 1)),
    )

    def sent(c, carry):
        whole(rows_ref, c, go_sem, come_sem).wait_send()
        whole(ret_ref, c, back_sem, home_sem).wait_send()
        to_left(c).wait_send()
        to_right(c).wait_send()
        return carry

    lax.fori_loop(0, chunks, sent, 0)


def rotary_tables(tokens, head_dim):
    half = head_dim // 2
    freqs = np.power(np.float32(10000.0), -np.arange(half, dtype=np.float32) / np.float32(half))
    angle = np.arange(tokens, dtype=np.float32)[:, None] * freqs[None, :].astype(np.float32)
    angle = np.tile(angle.astype(np.float64), (1, BLOCK // half))
    return np.cos(angle).astype(np.float32), np.sin(angle).astype(np.float32)


def body(
    state_tokens,
    gain_time,
    query_time,
    key_time,
    value_time,
    output_time,
    gain_space,
    query_space,
    key_space,
    value_space,
    output_space,
    neighbours,
):
    tokens, width = state_tokens.shape[1:]
    frames = lax.axis_size("frame")
    slab = 2 * BLOCK // frames
    chunks = tokens // (frames * slab)
    blocks = tokens // BLOCK
    head_dim = width // HEADS
    cosine, sine = rotary_tables(tokens, head_dim)
    vmem = pl.BlockSpec(memory_space=pltpu.VMEM)
    updated = pl.pallas_call(
        layer_kernel,
        out_shape=jax.ShapeDtypeStruct((tokens, width), BF16),
        in_specs=[pl.BlockSpec(memory_space=pltpu.SMEM)] + [vmem] * 13,
        out_specs=vmem,
        scratch_shapes=[
            pltpu.VMEM((chunks, frames, slab, width), BF16),
            pltpu.VMEM((chunks, frames, slab, width), BF16),
            pltpu.VMEM((chunks, frames, slab, width), BF16),
            pltpu.VMEM((3 * blocks, BLOCK, width), BF16),
            pltpu.VMEM((blocks, BLOCK, width), BF16),
            pltpu.VMEM((blocks, BLOCK, width), BF16),
            pltpu.VMEM((3 * blocks, BLOCK, width), BF16),
            pltpu.VMEM((3 * blocks, HEADS // 2, 2 * head_dim + 16, BLOCK), BF16),
            pltpu.VMEM((width, 2 * width), BF16),
            pltpu.VMEM((width, 2 * width), BF16),
            pltpu.VMEM((width, width), BF16),
            pltpu.VMEM((width, width), BF16),
            pltpu.VMEM((NEIGHBOUR_COUNT * BLOCK, width), BF16),
            pltpu.VMEM((NEIGHBOUR_COUNT * BLOCK, width), BF16),
            pltpu.VMEM((HEADS // 2, NEIGHBOUR_COUNT * BLOCK, 2 * BLOCK), F32),
            pltpu.VMEM((width, BLOCK), F32),
        ]
        + [pltpu.SemaphoreType.DMA((chunks,))] * 8,
        compiler_params=pltpu.CompilerParams(
            vmem_limit_bytes=48 << 20, collective_id=1, has_side_effects=True
        ),
    )(
        neighbours,
        state_tokens.reshape(tokens, width),
        gain_time.reshape(1, width),
        query_time,
        key_time,
        value_time,
        output_time,
        gain_space.reshape(1, width),
        query_space,
        key_space,
        value_space,
        output_space,
        jnp.asarray(cosine),
        jnp.asarray(sine),
    )
    return updated.reshape(state_tokens.shape)


def solution(mesh):
    return jax.shard_map(
        body,
        mesh=mesh,
        in_specs=(P("frame", "tile", None),) + (P(),) * 10 + (P("tile", None),),
        out_specs=P("frame", "tile", None),
        check_vma=False,
    )
```

```python
import functools
import math

import jax
import jax.numpy as jnp
import numpy as np
from jax import lax
from jax.experimental import pallas as pl
from jax.experimental.pallas import tpu as pltpu
from jax.sharding import PartitionSpec as P

HEADS = 8
BLOCK = 128
NEIGHBOUR_COUNT = 9
EPS = 1e-05
ROT_PERIOD = 1024
NEG = -1e30
F32 = jnp.float32
BF16 = jnp.bfloat16
MESH = pl.DeviceIdType.MESH


def nt(a, b):
    return lax.dot_general(a, b, (((1,), (1,)), ((), ())), preferred_element_type=F32)


def nn(a, b):
    return lax.dot_general(a, b, (((1,), (0,)), ((), ())), preferred_element_type=F32)


def rms(values, gain):
    square_mean = jnp.mean(values * values, axis=-1, keepdims=True)
    return values * lax.rsqrt(square_mean + EPS) * gain


def head_pair(rows, pair, head_dim):
    lane_head = lax.broadcasted_iota(jnp.int32, rows.shape, 1) // head_dim
    zero = jnp.zeros_like(rows)
    return jnp.concatenate(
        [jnp.where(lane_head == 2 * pair + k, rows, zero) for k in range(2)], axis=0
    )


def pair_result(total, head_dim, count):
    inverse = 1.0 / total[2 * head_dim : 2 * head_dim + 1, :]
    scaled = total[: 2 * head_dim, :] * inverse
    return jnp.concatenate(
        [scaled[:head_dim, :count], scaled[head_dim:, count:]], axis=0
    )


def time_chunk(slots, gain, wq, wk, wv_t, same, scale, head_dim):
    frames, tokens, width = slots.shape
    step = tokens // 2
    normed = rms(slots.astype(F32), gain)
    rows = jnp.concatenate(
        [
            normed[:, k * step : (k + 1) * step].reshape(BLOCK, width).astype(BF16)
            for k in range(2)
        ],
        axis=0,
    )
    query = (nn(rows, wq) * scale).astype(BF16)
    key = nn(rows, wk).astype(BF16)
    value_t = nt(wv_t, rows).astype(BF16)
    ones = jnp.ones((16, BLOCK), BF16)
    units = [(k, pair) for k in range(2) for pair in range(HEADS // 2)]
    scores = {}
    for k, pair in units:
        part = slice(k * BLOCK, (k + 1) * BLOCK)
        scores[k, pair] = jnp.where(
            same, nt(key[part], head_pair(query[part], pair, head_dim)), NEG
        )
    weights = {
        unit: jnp.exp2(value - jnp.max(value, axis=0, keepdims=True)).astype(BF16)
        for unit, value in scores.items()
    }
    halves = []
    for k in range(2):
        parts = []
        for pair in range(HEADS // 2):
            low = 2 * pair * head_dim
            held = jnp.concatenate(
                [value_t[low : low + 2 * head_dim, k * BLOCK : (k + 1) * BLOCK], ones], axis=0
            )
            parts.append(pair_result(nn(held, weights[k, pair]), head_dim, BLOCK))
        halves.append(jnp.concatenate(parts, axis=0).T.reshape(frames, step, width))
    return jnp.concatenate(halves, axis=1)


def swapped(weight):
    wide = weight.astype(F32)
    width = wide.shape[1]
    half = width // HEADS // 2
    lane = lax.broadcasted_iota(jnp.int32, wide.shape, 1)
    ahead = pltpu.roll(wide, width - half, 1)
    behind = pltpu.roll(wide, half, 1)
    return jnp.where(lane % (2 * half) < half, -ahead, behind).astype(BF16)


def layer_kernel(
    nbr_ref,
    state_hbm,
    gain_t_hbm,
    wqt_hbm,
    wkt_hbm,
    wvt_in_hbm,
    wt_hbm,
    gain_hbm,
    wq_hbm,
    wk_hbm,
    wv_hbm,
    wo_hbm,
    cos_hbm,
    sin_hbm,
    out_hbm,
    state_ref,
    gain_t_ref,
    wqt_ref,
    wkt_ref,
    wvt_in_ref,
    wt_ref,
    gain_ref,
    wq_ref,
    wk_ref,
    wv_ref,
    wo_ref,
    cos_ref,
    sin_ref,
    load_sem,
    out_ref,
    out_sem,
    rows_ref,
    attn_ref,
    ret_ref,
    norm_ref,
    mid_ref,
    q_ref,
    k_ref,
    v_ref,
    wq2_ref,
    wk2_ref,
    wvt_ref,
    wvtt_ref,
    kca_ref,
    kcb_ref,
    s_ref,
    att_ref,
    go_sem,
    come_sem,
    back_sem,
    home_sem,
    send_l,
    recv_l,
    send_r,
    recv_r,
):
    blocks = mid_ref.shape[0]
    width = state_ref.shape[-1]
    sources = (state_hbm, gain_t_hbm, wqt_hbm, wkt_hbm, wvt_in_hbm, wt_hbm, gain_hbm, wq_hbm, wk_hbm, wv_hbm, wo_hbm, cos_hbm, sin_hbm)
    targets = (state_ref, gain_t_ref, wqt_ref, wkt_ref, wvt_in_ref, wt_ref, gain_ref, wq_ref, wk_ref, wv_ref, wo_ref, cos_ref, sin_ref)
    loads = [
        pltpu.make_async_copy(source, target, load_sem.at[i])
        for i, (source, target) in enumerate(zip(sources, targets))
    ]
    head_dim = width // HEADS
    scale = math.log2(math.e) / math.sqrt(head_dim)
    chunks, frames, slab, _ = rows_ref.shape
    half = frames // 2
    per = blocks // chunks
    tile = lax.axis_index("tile")
    tiles = lax.axis_size("tile")
    left = lax.rem(tile + tiles - 1, tiles)
    right = lax.rem(tile + 1, tiles)
    me = lax.axis_index("frame")
    my_side = me // half
    my_place = lax.rem(me, half)

    def peer_at(k):
        return lax.rem(my_side + k // half, 2) * half + lax.rem(my_place + lax.rem(k, half), half)

    def mirror(k):
        return (k // half) * half + lax.rem(half - lax.rem(k, half), half)

    barrier = pltpu.get_barrier_semaphore()

    def greet(k, carry):
        pl.semaphore_signal(
            barrier, inc=1, device_id={"frame": peer_at(k)}, device_id_type=MESH
        )
        return carry

    lax.fori_loop(1, frames, greet, 0)
    for peer in (left, right):
        pl.semaphore_signal(barrier, inc=1, device_id={"tile": peer}, device_id_type=MESH)

    def go(c, k):
        at = pl.ds(pl.multiple_of((c * frames + peer_at(k)) * slab, slab), slab)
        return pltpu.make_async_remote_copy(
            src_ref=state_hbm.at[at, :],
            dst_ref=rows_ref.at[c, mirror(k)],
            send_sem=go_sem.at[c],
            recv_sem=come_sem.at[c],
            device_id={"frame": peer_at(k)},
            device_id_type=MESH,
        )

    def back(c, k):
        return pltpu.make_async_remote_copy(
            src_ref=attn_ref.at[c, k],
            dst_ref=ret_ref.at[c, me],
            send_sem=back_sem.at[c],
            recv_sem=home_sem.at[c],
            device_id={"frame": peer_at(k)},
            device_id_type=MESH,
        )

    def whole(ref, c, send_sem, recv_sem):
        return pltpu.make_async_remote_copy(
            src_ref=ref.at[c, pl.ds(0, frames - 1)],
            dst_ref=ref.at[c, pl.ds(0, frames - 1)],
            send_sem=send_sem.at[c],
            recv_sem=recv_sem.at[c],
            device_id={"frame": peer_at(1)},
            device_id_type=MESH,
        )

    def to_left(c):
        return pltpu.make_async_remote_copy(
            src_ref=norm_ref.at[pl.ds(blocks + per * c, per)],
            dst_ref=norm_ref.at[pl.ds(2 * blocks + per * c, per)],
            send_sem=send_l.at[c],
            recv_sem=recv_l.at[c],
            device_id={"tile": left},
            device_id_type=MESH,
        )

    def to_right(c):
        return pltpu.make_async_remote_copy(
            src_ref=norm_ref.at[pl.ds(blocks + per * c, per)],
            dst_ref=norm_ref.at[pl.ds(per * c, per)],
            send_sem=send_r.at[c],
            recv_sem=recv_r.at[c],
            device_id={"tile": right},
            device_id_type=MESH,
        )

    for load in loads:
        load.start()
    pl.semaphore_wait(barrier, frames + 1)

    def leave(c, carry):
        def one(i, inner):
            go(c, frames - 1 - i).start()
            return inner

        return lax.fori_loop(0, frames - 1, one, carry)

    lax.fori_loop(0, chunks, leave, 0)

    for load in loads:
        load.wait()

    def stay(c, carry):
        at = pl.ds(pl.multiple_of((c * frames + me) * slab, slab), slab)
        rows_ref[c, 0] = state_ref[at, :]
        return carry

    lax.fori_loop(0, chunks, stay, 0)
    wvtt_ref[...] = wvt_in_ref[...].astype(F32).T.astype(BF16)
    wq2_ref[:, :width] = wq_ref[...]
    wq2_ref[:, width:] = swapped(wq_ref[...])
    wk2_ref[:, :width] = wk_ref[...]
    wk2_ref[:, width:] = swapped(wk_ref[...])
    wvt_ref[...] = wv_ref[...].astype(F32).T.astype(BF16)


    row = lax.broadcasted_iota(jnp.int32, (BLOCK, 2 * BLOCK), 0)
    column = lax.broadcasted_iota(jnp.int32, (BLOCK, 2 * BLOCK), 1)
    step = slab // 2
    same = (row % step) == (column % step)

    def over_time(c, carry):
        whole(rows_ref, c, go_sem, come_sem).wait_recv()
        attended = time_chunk(
            rows_ref[c],
            gain_t_ref[...],
            wqt_ref[...],
            wkt_ref[...],
            wvtt_ref[...],
            same,
            scale,
            head_dim,
        )
        attn_ref[c] = attended.astype(BF16)

        def one(i, inner):
            back(c, frames - 1 - i).start()
            return inner

        lax.fori_loop(0, frames - 1, one, 0)
        ret_ref[c, me] = attn_ref[c, 0]
        return carry

    lax.fori_loop(0, chunks, over_time, 0)

    def turn(rows, weight_ref, j):
        at = pl.ds(pl.multiple_of(j * BLOCK, BLOCK), 2 * BLOCK)
        cosine = jnp.concatenate([cos_ref[at, :]] * 2, axis=1)
        sine = jnp.concatenate([sin_ref[at, :]] * 2, axis=1)
        both = nn(rows, weight_ref[...])
        return both[:, :width] * cosine + both[:, width:] * sine

    ones = jnp.ones((16, BLOCK), BF16)

    def key_value(g, j):
        rows = norm_ref[pl.ds(g, 2)].reshape(2 * BLOCK, width)
        k_ref[pl.ds(g, 2)] = turn(rows, wk2_ref, j).astype(BF16).reshape(2, BLOCK, width)
        value_t = nt(wvt_ref[...], rows).astype(BF16)
        for pair in range(HEADS // 2):
            low = 2 * pair * head_dim
            for k in range(2):
                v_ref[g + k, pair] = jnp.concatenate(
                    [value_t[low : low + 2 * head_dim, k * BLOCK : (k + 1) * BLOCK], ones], axis=0
                )

    gain = gain_ref[...]

    def own(c, carry):
        j = per * c
        whole(ret_ref, c, back_sem, home_sem).wait_recv()
        at = pl.ds(pl.multiple_of(c * frames * slab, frames * slab), frames * slab)
        returned = ret_ref[c].reshape(frames * slab, width)
        mid = (state_ref[at, :].astype(F32) + nn(returned, wt_ref[...])).astype(BF16)
        mid_ref[pl.ds(j, per)] = mid.reshape(per, BLOCK, width)
        rows = rms(mid.astype(F32), gain).astype(BF16)
        norm_ref[pl.ds(blocks + j, per)] = rows.reshape(per, BLOCK, width)
        to_left(c).start()
        to_right(c).start()
        query = (turn(rows, wq2_ref, j) * scale).astype(BF16)
        q_ref[pl.ds(j, per)] = query.reshape(per, BLOCK, width)
        key_value(blocks + j, j)
        return carry

    lax.fori_loop(0, chunks, own, 0)

    first = (tile - 1) * blocks
    total_blocks = tiles * blocks

    def place(b, m):
        entry = nbr_ref[b, m]
        offset = entry - first
        offset = jnp.where(offset < 0, offset + total_blocks, offset)
        offset = jnp.where(offset >= total_blocks, offset - total_blocks, offset)
        offset = jnp.minimum(offset, 3 * blocks - 1)
        return jnp.where(entry < 0, blocks + b, offset)

    def places(b):
        return [place(b, m) for m in range(NEIGHBOUR_COUNT)]

    last_rows = (NEIGHBOUR_COUNT - 1) * BLOCK

    def bias_of(b):
        return jnp.where(nbr_ref[b, NEIGHBOUR_COUNT - 1] < 0, NEG, 0.0).astype(F32)

    def fill(kc_ref, at):
        for m in range(NEIGHBOUR_COUNT):
            kc_ref[m * BLOCK : (m + 1) * BLOCK, :] = k_ref[at[m]]

    def score(kc_ref, query, pair, bias):
        scores = nt(kc_ref[...], head_pair(query, pair, head_dim))
        tail = scores[last_rows:] + bias
        s_ref[pair, :last_rows, :] = scores[:last_rows]
        s_ref[pair, last_rows:, :] = tail
        return jnp.maximum(
            jnp.max(scores[:last_rows], axis=0, keepdims=True),
            jnp.max(tail, axis=0, keepdims=True),
        )

    def weigh(at, pair, top):
        weights = jnp.exp2(s_ref[pair] - top).astype(BF16)
        held = jnp.concatenate([v_ref[g, pair] for g in at], axis=1)
        low = 2 * pair * head_dim
        att_ref[low : low + 2 * head_dim, :] = pair_result(nn(held, weights), head_dim, BLOCK)

    def arrive(c, carry):
        to_left(c).wait_recv()
        key_value(2 * blocks + per * c, per * c)
        to_right(c).wait_recv()
        key_value(per * c, per * c)
        return carry

    lax.fori_loop(0, chunks, arrive, 0)

    def deliver(b):
        at = pl.ds(pl.multiple_of(b * BLOCK, BLOCK), BLOCK)
        return pltpu.make_async_copy(out_ref.at[b], out_hbm.at[at, :], out_sem.at[b])

    def attend(b, tops):
        here = places(b)
        after = jnp.minimum(b + 1, blocks - 1)
        there = places(after)
        query = q_ref[b]
        bias = bias_of(b)
        fill(kca_ref, there)
        query_after = q_ref[after]
        bias_after = bias_of(after)
        late = [score(kcb_ref, query, 2, bias)]
        weigh(here, 0, tops[0])
        late.append(score(kcb_ref, query, 3, bias))
        weigh(here, 1, tops[1])
        fill(kcb_ref, there)
        early = [score(kca_ref, query_after, 0, bias_after)]
        weigh(here, 2, late[0])
        early.append(score(kca_ref, query_after, 1, bias_after))
        weigh(here, 3, late[1])
        early = tuple(early)
        attended = att_ref[...].T.astype(BF16)
        out_ref[b] = (mid_ref[b].astype(F32) + nn(attended, wo_ref[...])).astype(BF16)
        deliver(b).start()
        return early

    at_first = places(0)
    fill(kca_ref, at_first)
    fill(kcb_ref, at_first)
    query_first = q_ref[0]
    bias_first = bias_of(0)
    lax.fori_loop(
        0,
        blocks,
        attend,
        tuple(score(kca_ref, query_first, pair, bias_first) for pair in (0, 1)),
    )

    def sent(c, carry):
        whole(rows_ref, c, go_sem, come_sem).wait_send()
        whole(ret_ref, c, back_sem, home_sem).wait_send()
        to_left(c).wait_send()
        to_right(c).wait_send()
        return carry

    lax.fori_loop(0, chunks, sent, 0)

    def delivered(b, carry):
        deliver(b).wait()
        return carry

    lax.fori_loop(0, blocks, delivered, 0)


def rotary_tables(tokens, head_dim):
    half = head_dim // 2
    freqs = np.power(np.float32(10000.0), -np.arange(half, dtype=np.float32) / np.float32(half))
    angle = np.arange(tokens, dtype=np.float32)[:, None] * freqs[None, :].astype(np.float32)
    angle = np.tile(angle.astype(np.float64), (1, BLOCK // half))
    return np.cos(angle).astype(np.float32), np.sin(angle).astype(np.float32)


def body(
    state_tokens,
    gain_time,
    query_time,
    key_time,
    value_time,
    output_time,
    gain_space,
    query_space,
    key_space,
    value_space,
    output_space,
    neighbours,
):
    tokens, width = state_tokens.shape[1:]
    frames = lax.axis_size("frame")
    slab = 2 * BLOCK // frames
    chunks = tokens // (frames * slab)
    blocks = tokens // BLOCK
    head_dim = width // HEADS
    cosine, sine = rotary_tables(tokens, head_dim)
    updated = pl.pallas_call(
        layer_kernel,
        out_shape=jax.ShapeDtypeStruct((tokens, width), BF16),
        in_specs=[pl.BlockSpec(memory_space=pltpu.SMEM)] + [pl.BlockSpec(memory_space=pltpu.HBM)] * 13,
        out_specs=pl.BlockSpec(memory_space=pltpu.HBM),
        scratch_shapes=[
            pltpu.VMEM((tokens, width), BF16),
            pltpu.VMEM((1, width), F32),
            pltpu.VMEM((width, width), BF16),
            pltpu.VMEM((width, width), BF16),
            pltpu.VMEM((width, width), BF16),
            pltpu.VMEM((width, width), BF16),
            pltpu.VMEM((1, width), F32),
            pltpu.VMEM((width, width), BF16),
            pltpu.VMEM((width, width), BF16),
            pltpu.VMEM((width, width), BF16),
            pltpu.VMEM((width, width), BF16),
            pltpu.VMEM((tokens, BLOCK), F32),
            pltpu.VMEM((tokens, BLOCK), F32),
            pltpu.SemaphoreType.DMA((13,)),
            pltpu.VMEM((blocks, BLOCK, width), BF16),
            pltpu.SemaphoreType.DMA((blocks,)),
            pltpu.VMEM((chunks, frames, slab, width), BF16),
            pltpu.VMEM((chunks, frames, slab, width), BF16),
            pltpu.VMEM((chunks, frames, slab, width), BF16),
            pltpu.VMEM((3 * blocks, BLOCK, width), BF16),
            pltpu.VMEM((blocks, BLOCK, width), BF16),
            pltpu.VMEM((blocks, BLOCK, width), BF16),
            pltpu.VMEM((3 * blocks, BLOCK, width), BF16),
            pltpu.VMEM((3 * blocks, HEADS // 2, 2 * head_dim + 16, BLOCK), BF16),
            pltpu.VMEM((width, 2 * width), BF16),
            pltpu.VMEM((width, 2 * width), BF16),
            pltpu.VMEM((width, width), BF16),
            pltpu.VMEM((width, width), BF16),
            pltpu.VMEM((NEIGHBOUR_COUNT * BLOCK, width), BF16),
            pltpu.VMEM((NEIGHBOUR_COUNT * BLOCK, width), BF16),
            pltpu.VMEM((HEADS // 2, NEIGHBOUR_COUNT * BLOCK, 2 * BLOCK), F32),
            pltpu.VMEM((width, BLOCK), F32),
        ]
        + [pltpu.SemaphoreType.DMA((chunks,))] * 8,
        compiler_params=pltpu.CompilerParams(
            vmem_limit_bytes=67043328, collective_id=1, has_side_effects=True
        ),
    )(
        neighbours,
        state_tokens.reshape(tokens, width),
        gain_time.reshape(1, width),
        query_time,
        key_time,
        value_time,
        output_time,
        gain_space.reshape(1, width),
        query_space,
        key_space,
        value_space,
        output_space,
        jnp.asarray(cosine),
        jnp.asarray(sine),
    )
    return updated.reshape(state_tokens.shape)


def solution(mesh):
    return jax.shard_map(
        body,
        mesh=mesh,
        in_specs=(P("frame", "tile", None),) + (P(),) * 10 + (P("tile", None),),
        out_specs=P("frame", "tile", None),
        check_vma=False,
    )
```

```python
import functools
import math

import jax
import jax.numpy as jnp
import numpy as np
from jax import lax
from jax.experimental import pallas as pl
from jax.experimental.pallas import tpu as pltpu
from jax.sharding import PartitionSpec as P

HEADS = 8
BLOCK = 128
NEIGHBOUR_COUNT = 9
EPS = 1e-05
ROT_PERIOD = 1024
NEG = -1e30
F32 = jnp.float32
BF16 = jnp.bfloat16
MESH = pl.DeviceIdType.MESH


def nt(a, b):
    return lax.dot_general(a, b, (((1,), (1,)), ((), ())), preferred_element_type=F32)


def nn(a, b):
    return lax.dot_general(a, b, (((1,), (0,)), ((), ())), preferred_element_type=F32)


def rms(values, gain):
    square_mean = jnp.mean(values * values, axis=-1, keepdims=True)
    return values * lax.rsqrt(square_mean + EPS) * gain


def head_pair(rows, pair, head_dim):
    lane_head = lax.broadcasted_iota(jnp.int32, rows.shape, 1) // head_dim
    zero = jnp.zeros_like(rows)
    return jnp.concatenate(
        [jnp.where(lane_head == 2 * pair + k, rows, zero) for k in range(2)], axis=0
    )


def pair_result(total, head_dim, count):
    inverse = 1.0 / total[2 * head_dim : 2 * head_dim + 1, :]
    scaled = total[: 2 * head_dim, :] * inverse
    return jnp.concatenate(
        [scaled[:head_dim, :count], scaled[head_dim:, count:]], axis=0
    )


def time_chunk(slots, gain, wq, wk, wv_t, same, scale, head_dim):
    frames, tokens, width = slots.shape
    step = tokens // 2
    normed = rms(slots.astype(F32), gain)
    rows = jnp.concatenate(
        [
            normed[:, k * step : (k + 1) * step].reshape(BLOCK, width).astype(BF16)
            for k in range(2)
        ],
        axis=0,
    )
    query = (nn(rows, wq) * scale).astype(BF16)
    key = nn(rows, wk).astype(BF16)
    value_t = nt(wv_t, rows).astype(BF16)
    ones = jnp.ones((16, BLOCK), BF16)
    units = [(k, pair) for k in range(2) for pair in range(HEADS // 2)]
    scores = {}
    for k, pair in units:
        part = slice(k * BLOCK, (k + 1) * BLOCK)
        scores[k, pair] = jnp.where(
            same, nt(key[part], head_pair(query[part], pair, head_dim)), NEG
        )
    weights = {
        unit: jnp.exp2(value - jnp.max(value, axis=0, keepdims=True)).astype(BF16)
        for unit, value in scores.items()
    }
    halves = []
    for k in range(2):
        parts = []
        for pair in range(HEADS // 2):
            low = 2 * pair * head_dim
            held = jnp.concatenate(
                [value_t[low : low + 2 * head_dim, k * BLOCK : (k + 1) * BLOCK], ones], axis=0
            )
            parts.append(pair_result(nn(held, weights[k, pair]), head_dim, BLOCK))
        halves.append(jnp.concatenate(parts, axis=0).T.reshape(frames, step, width))
    return jnp.concatenate(halves, axis=1)


def swapped(weight):
    wide = weight.astype(F32)
    width = wide.shape[1]
    half = width // HEADS // 2
    lane = lax.broadcasted_iota(jnp.int32, wide.shape, 1)
    ahead = pltpu.roll(wide, width - half, 1)
    behind = pltpu.roll(wide, half, 1)
    return jnp.where(lane % (2 * half) < half, -ahead, behind).astype(BF16)


def layer_kernel(
    nbr_ref,
    state_hbm,
    gain_t_hbm,
    wqt_hbm,
    wkt_hbm,
    wvt_in_hbm,
    wt_hbm,
    gain_hbm,
    wq_hbm,
    wk_hbm,
    wv_hbm,
    wo_hbm,
    cos_hbm,
    sin_hbm,
    out_hbm,
    state_ref,
    gain_t_ref,
    wqt_ref,
    wkt_ref,
    wvt_in_ref,
    wt_ref,
    gain_ref,
    wq_ref,
    wk_ref,
    wv_ref,
    wo_ref,
    cos_ref,
    sin_ref,
    load_sem,
    out_ref,
    out_sem,
    rows_ref,
    attn_ref,
    ret_ref,
    norm_ref,
    mid_ref,
    q_ref,
    k_ref,
    v_ref,
    wq2_ref,
    wk2_ref,
    wvt_ref,
    wvtt_ref,
    kca_ref,
    kcb_ref,
    s_ref,
    att_ref,
    go_sem,
    come_sem,
    back_sem,
    home_sem,
    send_l,
    recv_l,
    send_r,
    recv_r,
):
    blocks = mid_ref.shape[0]
    width = state_ref.shape[-1]
    sources = (state_hbm, gain_t_hbm, wqt_hbm, wkt_hbm, wvt_in_hbm, wt_hbm, gain_hbm, wq_hbm, wk_hbm, wv_hbm, wo_hbm, cos_hbm, sin_hbm)
    targets = (state_ref, gain_t_ref, wqt_ref, wkt_ref, wvt_in_ref, wt_ref, gain_ref, wq_ref, wk_ref, wv_ref, wo_ref, cos_ref, sin_ref)
    loads = [
        pltpu.make_async_copy(source, target, load_sem.at[i])
        for i, (source, target) in enumerate(zip(sources, targets))
    ]
    head_dim = width // HEADS
    scale = math.log2(math.e) / math.sqrt(head_dim)
    chunks, frames, slab, _ = rows_ref.shape
    half = frames // 2
    per = blocks // chunks
    tile = lax.axis_index("tile")
    tiles = lax.axis_size("tile")
    left = lax.rem(tile + tiles - 1, tiles)
    right = lax.rem(tile + 1, tiles)
    me = lax.axis_index("frame")
    my_side = me // half
    my_place = lax.rem(me, half)

    def peer_at(k):
        return lax.rem(my_side + k // half, 2) * half + lax.rem(my_place + lax.rem(k, half), half)

    def mirror(k):
        return (k // half) * half + lax.rem(half - lax.rem(k, half), half)

    barrier = pltpu.get_barrier_semaphore()

    def greet(k, carry):
        pl.semaphore_signal(
            barrier, inc=1, device_id={"frame": peer_at(k)}, device_id_type=MESH
        )
        return carry

    lax.fori_loop(1, frames, greet, 0)
    for peer in (left, right):
        pl.semaphore_signal(barrier, inc=1, device_id={"tile": peer}, device_id_type=MESH)

    def go(c, k):
        at = pl.ds(pl.multiple_of((c * frames + peer_at(k)) * slab, slab), slab)
        return pltpu.make_async_remote_copy(
            src_ref=state_hbm.at[at, :],
            dst_ref=rows_ref.at[c, mirror(k)],
            send_sem=go_sem.at[c],
            recv_sem=come_sem.at[c],
            device_id={"frame": peer_at(k)},
            device_id_type=MESH,
        )

    def back(c, k):
        return pltpu.make_async_remote_copy(
            src_ref=attn_ref.at[c, k],
            dst_ref=ret_ref.at[c, me],
            send_sem=back_sem.at[c],
            recv_sem=home_sem.at[c],
            device_id={"frame": peer_at(k)},
            device_id_type=MESH,
        )

    def whole(ref, c, send_sem, recv_sem):
        return pltpu.make_async_remote_copy(
            src_ref=ref.at[c, pl.ds(0, frames - 1)],
            dst_ref=ref.at[c, pl.ds(0, frames - 1)],
            send_sem=send_sem.at[c],
            recv_sem=recv_sem.at[c],
            device_id={"frame": peer_at(1)},
            device_id_type=MESH,
        )

    def to_left(c):
        return pltpu.make_async_remote_copy(
            src_ref=norm_ref.at[pl.ds(blocks + per * c, per)],
            dst_ref=norm_ref.at[pl.ds(2 * blocks + per * c, per)],
            send_sem=send_l.at[c],
            recv_sem=recv_l.at[c],
            device_id={"tile": left},
            device_id_type=MESH,
        )

    def to_right(c):
        return pltpu.make_async_remote_copy(
            src_ref=norm_ref.at[pl.ds(blocks + per * c, per)],
            dst_ref=norm_ref.at[pl.ds(per * c, per)],
            send_sem=send_r.at[c],
            recv_sem=recv_r.at[c],
            device_id={"tile": right},
            device_id_type=MESH,
        )

    for load in loads:
        load.start()
    pl.semaphore_wait(barrier, frames + 1)

    def leave(c, carry):
        def one(i, inner):
            go(c, frames - 1 - i).start()
            return inner

        return lax.fori_loop(0, frames - 1, one, carry)

    lax.fori_loop(0, chunks, leave, 0)

    for load in loads:
        load.wait()

    def stay(c, carry):
        at = pl.ds(pl.multiple_of((c * frames + me) * slab, slab), slab)
        rows_ref[c, 0] = state_ref[at, :]
        return carry

    lax.fori_loop(0, chunks, stay, 0)
    wvtt_ref[...] = wvt_in_ref[...].astype(F32).T.astype(BF16)
    wq2_ref[:, :width] = wq_ref[...]
    wq2_ref[:, width:] = swapped(wq_ref[...])
    wk2_ref[:, :width] = wk_ref[...]
    wk2_ref[:, width:] = swapped(wk_ref[...])
    wvt_ref[...] = wv_ref[...].astype(F32).T.astype(BF16)


    row = lax.broadcasted_iota(jnp.int32, (BLOCK, 2 * BLOCK), 0)
    column = lax.broadcasted_iota(jnp.int32, (BLOCK, 2 * BLOCK), 1)
    step = slab // 2
    same = (row % step) == (column % step)

    def over_time(c, carry):
        whole(rows_ref, c, go_sem, come_sem).wait_recv()
        attended = time_chunk(
            rows_ref[c],
            gain_t_ref[...],
            wqt_ref[...],
            wkt_ref[...],
            wvtt_ref[...],
            same,
            scale,
            head_dim,
        )
        attn_ref[c] = attended.astype(BF16)

        def one(i, inner):
            back(c, frames - 1 - i).start()
            return inner

        lax.fori_loop(0, frames - 1, one, 0)
        ret_ref[c, me] = attn_ref[c, 0]
        return carry

    lax.fori_loop(0, chunks, over_time, 0)

    def turn(rows, weight_ref, j):
        at = pl.ds(pl.multiple_of(j * BLOCK, BLOCK), 2 * BLOCK)
        cosine = jnp.concatenate([cos_ref[at, :]] * 2, axis=1)
        sine = jnp.concatenate([sin_ref[at, :]] * 2, axis=1)
        both = nn(rows, weight_ref[...])
        return both[:, :width] * cosine + both[:, width:] * sine

    ones = jnp.ones((16, BLOCK), BF16)

    def key_value(g, j):
        rows = norm_ref[pl.ds(g, 2)].reshape(2 * BLOCK, width)
        k_ref[pl.ds(g, 2)] = turn(rows, wk2_ref, j).astype(BF16).reshape(2, BLOCK, width)
        value_t = nt(wvt_ref[...], rows).astype(BF16)
        for pair in range(HEADS // 2):
            low = 2 * pair * head_dim
            for k in range(2):
                v_ref[g + k, pair] = jnp.concatenate(
                    [value_t[low : low + 2 * head_dim, k * BLOCK : (k + 1) * BLOCK], ones], axis=0
                )

    def arrive(c, carry):
        to_left(c).wait_recv()
        key_value(2 * blocks + per * c, per * c)
        to_right(c).wait_recv()
        key_value(per * c, per * c)
        return carry

    gain = gain_ref[...]

    def own(c, carry):
        j = per * c
        lax.fori_loop(0, jnp.where(c == chunks - 1, 1, 0), arrive, 0)
        whole(ret_ref, c, back_sem, home_sem).wait_recv()
        at = pl.ds(pl.multiple_of(c * frames * slab, frames * slab), frames * slab)
        returned = ret_ref[c].reshape(frames * slab, width)
        mid = (state_ref[at, :].astype(F32) + nn(returned, wt_ref[...])).astype(BF16)
        mid_ref[pl.ds(j, per)] = mid.reshape(per, BLOCK, width)
        rows = rms(mid.astype(F32), gain).astype(BF16)
        norm_ref[pl.ds(blocks + j, per)] = rows.reshape(per, BLOCK, width)
        to_left(c).start()
        to_right(c).start()
        query = (turn(rows, wq2_ref, j) * scale).astype(BF16)
        q_ref[pl.ds(j, per)] = query.reshape(per, BLOCK, width)
        key_value(blocks + j, j)
        return carry

    lax.fori_loop(0, chunks, own, 0)

    first = (tile - 1) * blocks
    total_blocks = tiles * blocks

    def place(b, m):
        entry = nbr_ref[b, m]
        offset = entry - first
        offset = jnp.where(offset < 0, offset + total_blocks, offset)
        offset = jnp.where(offset >= total_blocks, offset - total_blocks, offset)
        offset = jnp.minimum(offset, 3 * blocks - 1)
        return jnp.where(entry < 0, blocks + b, offset)

    def places(b):
        return [place(b, m) for m in range(NEIGHBOUR_COUNT)]

    last_rows = (NEIGHBOUR_COUNT - 1) * BLOCK

    def bias_of(b):
        return jnp.where(nbr_ref[b, NEIGHBOUR_COUNT - 1] < 0, NEG, 0.0).astype(F32)

    def fill(kc_ref, at):
        for m in range(NEIGHBOUR_COUNT):
            kc_ref[m * BLOCK : (m + 1) * BLOCK, :] = k_ref[at[m]]

    def score(kc_ref, query, pair, bias):
        scores = nt(kc_ref[...], head_pair(query, pair, head_dim))
        tail = scores[last_rows:] + bias
        s_ref[pair, :last_rows, :] = scores[:last_rows]
        s_ref[pair, last_rows:, :] = tail
        return jnp.maximum(
            jnp.max(scores[:last_rows], axis=0, keepdims=True),
            jnp.max(tail, axis=0, keepdims=True),
        )

    def weigh(at, pair, top):
        weights = jnp.exp2(s_ref[pair] - top).astype(BF16)
        held = jnp.concatenate([v_ref[g, pair] for g in at], axis=1)
        low = 2 * pair * head_dim
        att_ref[low : low + 2 * head_dim, :] = pair_result(nn(held, weights), head_dim, BLOCK)

    lax.fori_loop(1, chunks, arrive, 0)

    def deliver(b):
        at = pl.ds(pl.multiple_of(b * BLOCK, BLOCK), BLOCK)
        return pltpu.make_async_copy(out_ref.at[b], out_hbm.at[at, :], out_sem.at[b])

    def attend(b, tops):
        here = places(b)
        after = jnp.minimum(b + 1, blocks - 1)
        there = places(after)
        query = q_ref[b]
        bias = bias_of(b)
        fill(kca_ref, there)
        query_after = q_ref[after]
        bias_after = bias_of(after)
        late = [score(kcb_ref, query, 2, bias)]
        weigh(here, 0, tops[0])
        early = [score(kca_ref, query_after, 0, bias_after)]
        late.append(score(kcb_ref, query, 3, bias))
        fill(kcb_ref, there)
        weigh(here, 1, tops[1])
        early.append(score(kca_ref, query_after, 1, bias_after))
        weigh(here, 2, late[0])
        weigh(here, 3, late[1])
        early = tuple(early)
        attended = att_ref[...].T.astype(BF16)
        out_ref[b] = (mid_ref[b].astype(F32) + nn(attended, wo_ref[...])).astype(BF16)
        deliver(b).start()
        return early

    at_first = places(0)
    fill(kca_ref, at_first)
    fill(kcb_ref, at_first)
    query_first = q_ref[0]
    bias_first = bias_of(0)
    lax.fori_loop(
        0,
        blocks,
        attend,
        tuple(score(kca_ref, query_first, pair, bias_first) for pair in (0, 1)),
        unroll=2,
    )

    def sent(c, carry):
        whole(rows_ref, c, go_sem, come_sem).wait_send()
        whole(ret_ref, c, back_sem, home_sem).wait_send()
        to_left(c).wait_send()
        to_right(c).wait_send()
        return carry

    lax.fori_loop(0, chunks, sent, 0)

    def delivered(b, carry):
        deliver(b).wait()
        return carry

    lax.fori_loop(0, blocks, delivered, 0)


def rotary_tables(tokens, head_dim):
    half = head_dim // 2
    freqs = np.power(np.float32(10000.0), -np.arange(half, dtype=np.float32) / np.float32(half))
    angle = np.arange(tokens, dtype=np.float32)[:, None] * freqs[None, :].astype(np.float32)
    angle = np.tile(angle.astype(np.float64), (1, BLOCK // half))
    return np.cos(angle).astype(np.float32), np.sin(angle).astype(np.float32)


def body(
    state_tokens,
    gain_time,
    query_time,
    key_time,
    value_time,
    output_time,
    gain_space,
    query_space,
    key_space,
    value_space,
    output_space,
    neighbours,
):
    tokens, width = state_tokens.shape[1:]
    frames = lax.axis_size("frame")
    slab = 2 * BLOCK // frames
    chunks = tokens // (frames * slab)
    blocks = tokens // BLOCK
    head_dim = width // HEADS
    cosine, sine = rotary_tables(tokens, head_dim)
    updated = pl.pallas_call(
        layer_kernel,
        out_shape=jax.ShapeDtypeStruct((tokens, width), BF16),
        in_specs=[pl.BlockSpec(memory_space=pltpu.SMEM)] + [pl.BlockSpec(memory_space=pltpu.HBM)] * 13,
        out_specs=pl.BlockSpec(memory_space=pltpu.HBM),
        scratch_shapes=[
            pltpu.VMEM((tokens, width), BF16),
            pltpu.VMEM((1, width), F32),
            pltpu.VMEM((width, width), BF16),
            pltpu.VMEM((width, width), BF16),
            pltpu.VMEM((width, width), BF16),
            pltpu.VMEM((width, width), BF16),
            pltpu.VMEM((1, width), F32),
            pltpu.VMEM((width, width), BF16),
            pltpu.VMEM((width, width), BF16),
            pltpu.VMEM((width, width), BF16),
            pltpu.VMEM((width, width), BF16),
            pltpu.VMEM((tokens, BLOCK), F32),
            pltpu.VMEM((tokens, BLOCK), F32),
            pltpu.SemaphoreType.DMA((13,)),
            pltpu.VMEM((blocks, BLOCK, width), BF16),
            pltpu.SemaphoreType.DMA((blocks,)),
            pltpu.VMEM((chunks, frames, slab, width), BF16),
            pltpu.VMEM((chunks, frames, slab, width), BF16),
            pltpu.VMEM((chunks, frames, slab, width), BF16),
            pltpu.VMEM((3 * blocks, BLOCK, width), BF16),
            pltpu.VMEM((blocks, BLOCK, width), BF16),
            pltpu.VMEM((blocks, BLOCK, width), BF16),
            pltpu.VMEM((3 * blocks, BLOCK, width), BF16),
            pltpu.VMEM((3 * blocks, HEADS // 2, 2 * head_dim + 16, BLOCK), BF16),
            pltpu.VMEM((width, 2 * width), BF16),
            pltpu.VMEM((width, 2 * width), BF16),
            pltpu.VMEM((width, width), BF16),
            pltpu.VMEM((width, width), BF16),
            pltpu.VMEM((NEIGHBOUR_COUNT * BLOCK, width), BF16),
            pltpu.VMEM((NEIGHBOUR_COUNT * BLOCK, width), BF16),
            pltpu.VMEM((HEADS // 2, NEIGHBOUR_COUNT * BLOCK, 2 * BLOCK), F32),
            pltpu.VMEM((width, BLOCK), F32),
        ]
        + [pltpu.SemaphoreType.DMA((chunks,))] * 8,
        compiler_params=pltpu.CompilerParams(
            vmem_limit_bytes=67043328, collective_id=1, has_side_effects=True
        ),
    )(
        neighbours,
        state_tokens.reshape(tokens, width),
        gain_time.reshape(1, width),
        query_time,
        key_time,
        value_time,
        output_time,
        gain_space.reshape(1, width),
        query_space,
        key_space,
        value_space,
        output_space,
        jnp.asarray(cosine),
        jnp.asarray(sine),
    )
    return updated.reshape(state_tokens.shape)


def solution(mesh):
    return jax.shard_map(
        body,
        mesh=mesh,
        in_specs=(P("frame", "tile", None),) + (P(),) * 10 + (P("tile", None),),
        out_specs=P("frame", "tile", None),
        check_vma=False,
    )
```

```python
import functools
import math

import jax
import jax.numpy as jnp
import numpy as np
from jax import lax
from jax.experimental import pallas as pl
from jax.experimental.pallas import tpu as pltpu
from jax.sharding import PartitionSpec as P

HEADS = 8
BLOCK = 128
NEIGHBOUR_COUNT = 9
EPS = 1e-05
ROT_PERIOD = 1024
NEG = -1e30
F32 = jnp.float32
BF16 = jnp.bfloat16
MESH = pl.DeviceIdType.MESH


def nt(a, b):
    return lax.dot_general(a, b, (((1,), (1,)), ((), ())), preferred_element_type=F32)


def nn(a, b):
    return lax.dot_general(a, b, (((1,), (0,)), ((), ())), preferred_element_type=F32)


def rms(values, gain):
    square_mean = jnp.mean(values * values, axis=-1, keepdims=True)
    return values * lax.rsqrt(square_mean + EPS) * gain


def head_pair(rows, pair, head_dim):
    lane_head = lax.broadcasted_iota(jnp.int32, rows.shape, 1) // head_dim
    zero = jnp.zeros_like(rows)
    return jnp.concatenate(
        [jnp.where(lane_head == 2 * pair + k, rows, zero) for k in range(2)], axis=0
    )


def pair_result(total, head_dim, count):
    inverse = 1.0 / total[2 * head_dim : 2 * head_dim + 1, :]
    scaled = total[: 2 * head_dim, :] * inverse
    return jnp.concatenate(
        [scaled[:head_dim, :count], scaled[head_dim:, count:]], axis=0
    )


def time_chunk(slots, gain, wq, wk, wv_t, same, scale, head_dim):
    frames, tokens, width = slots.shape
    step = tokens // 2
    normed = rms(slots.astype(F32), gain)
    rows = jnp.concatenate(
        [
            normed[:, k * step : (k + 1) * step].reshape(BLOCK, width).astype(BF16)
            for k in range(2)
        ],
        axis=0,
    )
    query = (nn(rows, wq) * scale).astype(BF16)
    key = nn(rows, wk).astype(BF16)
    value_t = nt(wv_t, rows).astype(BF16)
    ones = jnp.ones((16, BLOCK), BF16)
    units = [(k, pair) for k in range(2) for pair in range(HEADS // 2)]
    scores = {}
    for k, pair in units:
        part = slice(k * BLOCK, (k + 1) * BLOCK)
        scores[k, pair] = jnp.where(
            same, nt(key[part], head_pair(query[part], pair, head_dim)), NEG
        )
    weights = {
        unit: jnp.exp2(value - jnp.max(value, axis=0, keepdims=True)).astype(BF16)
        for unit, value in scores.items()
    }
    halves = []
    for k in range(2):
        parts = []
        for pair in range(HEADS // 2):
            low = 2 * pair * head_dim
            held = jnp.concatenate(
                [value_t[low : low + 2 * head_dim, k * BLOCK : (k + 1) * BLOCK], ones], axis=0
            )
            parts.append(pair_result(nn(held, weights[k, pair]), head_dim, BLOCK))
        halves.append(jnp.concatenate(parts, axis=0).T.reshape(frames, step, width))
    return jnp.concatenate(halves, axis=1)


def swapped(weight):
    wide = weight.astype(F32)
    width = wide.shape[1]
    half = width // HEADS // 2
    lane = lax.broadcasted_iota(jnp.int32, wide.shape, 1)
    ahead = pltpu.roll(wide, width - half, 1)
    behind = pltpu.roll(wide, half, 1)
    return jnp.where(lane % (2 * half) < half, -ahead, behind).astype(BF16)


def layer_kernel(
    nbr_ref,
    state_hbm,
    gain_t_hbm,
    wqt_hbm,
    wkt_hbm,
    wvt_in_hbm,
    wt_hbm,
    gain_hbm,
    wq_hbm,
    wk_hbm,
    wv_hbm,
    wo_hbm,
    cos_hbm,
    sin_hbm,
    out_hbm,
    state_ref,
    gain_t_ref,
    wqt_ref,
    wkt_ref,
    wvt_in_ref,
    wt_ref,
    gain_ref,
    wq_ref,
    wk_ref,
    wv_ref,
    wo_ref,
    cos_ref,
    sin_ref,
    load_sem,
    out_ref,
    out_sem,
    rows_ref,
    attn_ref,
    ret_ref,
    norm_ref,
    mid_ref,
    q_ref,
    k_ref,
    v_ref,
    wq2_ref,
    wk2_ref,
    wvt_ref,
    wvtt_ref,
    kca_ref,
    kcb_ref,
    s_ref,
    att_ref,
    go_sem,
    come_sem,
    back_sem,
    home_sem,
    send_l,
    recv_l,
    send_r,
    recv_r,
):
    blocks = mid_ref.shape[0]
    width = state_ref.shape[-1]
    sources = (state_hbm, gain_t_hbm, wqt_hbm, wkt_hbm, wvt_in_hbm, wt_hbm, gain_hbm, wq_hbm, wk_hbm, wv_hbm, wo_hbm, cos_hbm, sin_hbm)
    targets = (state_ref, gain_t_ref, wqt_ref, wkt_ref, wvt_in_ref, wt_ref, gain_ref, wq_ref, wk_ref, wv_ref, wo_ref, cos_ref, sin_ref)
    loads = [
        pltpu.make_async_copy(source, target, load_sem.at[i])
        for i, (source, target) in enumerate(zip(sources, targets))
    ]
    head_dim = width // HEADS
    scale = math.log2(math.e) / math.sqrt(head_dim)
    chunks, frames, slab, _ = rows_ref.shape
    half = frames // 2
    per = blocks // chunks
    tile = lax.axis_index("tile")
    tiles = lax.axis_size("tile")
    left = lax.rem(tile + tiles - 1, tiles)
    right = lax.rem(tile + 1, tiles)
    me = lax.axis_index("frame")
    my_side = me // half
    my_place = lax.rem(me, half)

    def peer_at(k):
        return lax.rem(my_side + k // half, 2) * half + lax.rem(my_place + lax.rem(k, half), half)

    def mirror(k):
        return (k // half) * half + lax.rem(half - lax.rem(k, half), half)

    barrier = pltpu.get_barrier_semaphore()

    def greet(k, carry):
        pl.semaphore_signal(
            barrier, inc=1, device_id={"frame": peer_at(k)}, device_id_type=MESH
        )
        return carry

    lax.fori_loop(1, frames, greet, 0)
    for peer in (left, right):
        pl.semaphore_signal(barrier, inc=1, device_id={"tile": peer}, device_id_type=MESH)

    def go(c, k):
        at = pl.ds(pl.multiple_of((c * frames + peer_at(k)) * slab, slab), slab)
        return pltpu.make_async_remote_copy(
            src_ref=state_hbm.at[at, :],
            dst_ref=rows_ref.at[c, mirror(k)],
            send_sem=go_sem.at[c],
            recv_sem=come_sem.at[c],
            device_id={"frame": peer_at(k)},
            device_id_type=MESH,
        )

    def back(c, k):
        return pltpu.make_async_remote_copy(
            src_ref=attn_ref.at[c, k],
            dst_ref=ret_ref.at[c, me],
            send_sem=back_sem.at[c],
            recv_sem=home_sem.at[c],
            device_id={"frame": peer_at(k)},
            device_id_type=MESH,
        )

    def whole(ref, c, send_sem, recv_sem):
        return pltpu.make_async_remote_copy(
            src_ref=ref.at[c, pl.ds(0, frames - 1)],
            dst_ref=ref.at[c, pl.ds(0, frames - 1)],
            send_sem=send_sem.at[c],
            recv_sem=recv_sem.at[c],
            device_id={"frame": peer_at(1)},
            device_id_type=MESH,
        )

    def to_left(c):
        return pltpu.make_async_remote_copy(
            src_ref=norm_ref.at[pl.ds(blocks + per * c, per)],
            dst_ref=norm_ref.at[pl.ds(2 * blocks + per * c, per)],
            send_sem=send_l.at[c],
            recv_sem=recv_l.at[c],
            device_id={"tile": left},
            device_id_type=MESH,
        )

    def to_right(c):
        return pltpu.make_async_remote_copy(
            src_ref=norm_ref.at[pl.ds(blocks + per * c, per)],
            dst_ref=norm_ref.at[pl.ds(per * c, per)],
            send_sem=send_r.at[c],
            recv_sem=recv_r.at[c],
            device_id={"tile": right},
            device_id_type=MESH,
        )

    for load in loads:
        load.start()
    pl.semaphore_wait(barrier, frames + 1)

    def leave(c, carry):
        def one(i, inner):
            go(c, frames - 1 - i).start()
            return inner

        return lax.fori_loop(0, frames - 1, one, carry)

    lax.fori_loop(0, chunks, leave, 0)

    for load in loads:
        load.wait()

    def stay(c, carry):
        at = pl.ds(pl.multiple_of((c * frames + me) * slab, slab), slab)
        rows_ref[c, 0] = state_ref[at, :]
        return carry

    lax.fori_loop(0, chunks, stay, 0)
    wvtt_ref[...] = wvt_in_ref[...].astype(F32).T.astype(BF16)
    wq2_ref[:, :width] = wq_ref[...]
    wq2_ref[:, width:] = swapped(wq_ref[...])
    wk2_ref[:, :width] = wk_ref[...]
    wk2_ref[:, width:] = swapped(wk_ref[...])
    wvt_ref[...] = wv_ref[...].astype(F32).T.astype(BF16)


    row = lax.broadcasted_iota(jnp.int32, (BLOCK, 2 * BLOCK), 0)
    column = lax.broadcasted_iota(jnp.int32, (BLOCK, 2 * BLOCK), 1)
    step = slab // 2
    same = (row % step) == (column % step)

    def over_time(c, carry):
        whole(rows_ref, c, go_sem, come_sem).wait_recv()
        attended = time_chunk(
            rows_ref[c],
            gain_t_ref[...],
            wqt_ref[...],
            wkt_ref[...],
            wvtt_ref[...],
            same,
            scale,
            head_dim,
        )
        attn_ref[c] = attended.astype(BF16)

        def one(i, inner):
            back(c, frames - 1 - i).start()
            return inner

        lax.fori_loop(0, frames - 1, one, 0)
        ret_ref[c, me] = attn_ref[c, 0]
        return carry

    lax.fori_loop(0, chunks, over_time, 0)

    def turn(rows, weight_ref, j):
        at = pl.ds(pl.multiple_of(j * BLOCK, BLOCK), 2 * BLOCK)
        cosine = jnp.concatenate([cos_ref[at, :]] * 2, axis=1)
        sine = jnp.concatenate([sin_ref[at, :]] * 2, axis=1)
        both = nn(rows, weight_ref[...])
        return both[:, :width] * cosine + both[:, width:] * sine

    ones = jnp.ones((16, BLOCK), BF16)

    def key_value(g, j):
        rows = norm_ref[pl.ds(g, 2)].reshape(2 * BLOCK, width)
        k_ref[pl.ds(g, 2)] = turn(rows, wk2_ref, j).astype(BF16).reshape(2, BLOCK, width)
        value_t = nt(wvt_ref[...], rows).astype(BF16)
        for pair in range(HEADS // 2):
            low = 2 * pair * head_dim
            for k in range(2):
                v_ref[g + k, pair] = jnp.concatenate(
                    [value_t[low : low + 2 * head_dim, k * BLOCK : (k + 1) * BLOCK], ones], axis=0
                )

    gain = gain_ref[...]

    def own(c, carry):
        j = per * c
        whole(ret_ref, c, back_sem, home_sem).wait_recv()
        at = pl.ds(pl.multiple_of(c * frames * slab, frames * slab), frames * slab)
        returned = ret_ref[c].reshape(frames * slab, width)
        mid = (state_ref[at, :].astype(F32) + nn(returned, wt_ref[...])).astype(BF16)
        mid_ref[pl.ds(j, per)] = mid.reshape(per, BLOCK, width)
        rows = rms(mid.astype(F32), gain).astype(BF16)
        norm_ref[pl.ds(blocks + j, per)] = rows.reshape(per, BLOCK, width)
        to_left(c).start()
        to_right(c).start()
        query = (turn(rows, wq2_ref, j) * scale).astype(BF16)
        q_ref[pl.ds(j, per)] = query.reshape(per, BLOCK, width)
        key_value(blocks + j, j)
        return carry

    lax.fori_loop(0, chunks, own, 0)

    first = (tile - 1) * blocks
    total_blocks = tiles * blocks

    def place(b, m):
        entry = nbr_ref[b, m]
        offset = entry - first
        offset = jnp.where(offset < 0, offset + total_blocks, offset)
        offset = jnp.where(offset >= total_blocks, offset - total_blocks, offset)
        offset = jnp.minimum(offset, 3 * blocks - 1)
        return jnp.where(entry < 0, blocks + b, offset)

    def places(b):
        return [place(b, m) for m in range(NEIGHBOUR_COUNT)]

    last_rows = (NEIGHBOUR_COUNT - 1) * BLOCK

    def bias_of(b):
        return jnp.where(nbr_ref[b, NEIGHBOUR_COUNT - 1] < 0, NEG, 0.0).astype(F32)

    def fill(kc_ref, at):
        for m in range(NEIGHBOUR_COUNT):
            kc_ref[m * BLOCK : (m + 1) * BLOCK, :] = k_ref[at[m]]

    def score(kc_ref, query, pair, bias):
        scores = nt(kc_ref[...], head_pair(query, pair, head_dim))
        tail = scores[last_rows:] + bias
        s_ref[pair, :last_rows, :] = scores[:last_rows]
        s_ref[pair, last_rows:, :] = tail
        return jnp.maximum(
            jnp.max(scores[:last_rows], axis=0, keepdims=True),
            jnp.max(tail, axis=0, keepdims=True),
        )

    def weigh(at, pair, top):
        weights = jnp.exp2(s_ref[pair] - top).astype(BF16)
        held = jnp.concatenate([v_ref[g, pair] for g in at], axis=1)
        low = 2 * pair * head_dim
        att_ref[low : low + 2 * head_dim, :] = pair_result(nn(held, weights), head_dim, BLOCK)

    def arrive(c, carry):
        to_left(c).wait_recv()
        key_value(2 * blocks + per * c, per * c)
        to_right(c).wait_recv()
        key_value(per * c, per * c)
        return carry

    lax.fori_loop(0, chunks, arrive, 0)

    def deliver(b):
        at = pl.ds(pl.multiple_of(b * BLOCK, BLOCK), BLOCK)
        return pltpu.make_async_copy(out_ref.at[b], out_hbm.at[at, :], out_sem.at[b])

    def attend(b, tops):
        here = places(b)
        after = jnp.minimum(b + 1, blocks - 1)
        there = places(after)
        query = q_ref[b]
        bias = bias_of(b)
        fill(kca_ref, there)
        query_after = q_ref[after]
        bias_after = bias_of(after)
        late = [score(kcb_ref, query, 2, bias)]
        weigh(here, 0, tops[0])
        early = [score(kca_ref, query_after, 0, bias_after)]
        late.append(score(kcb_ref, query, 3, bias))
        fill(kcb_ref, there)
        weigh(here, 1, tops[1])
        early.append(score(kca_ref, query_after, 1, bias_after))
        weigh(here, 2, late[0])
        weigh(here, 3, late[1])
        early = tuple(early)
        attended = att_ref[...].T.astype(BF16)
        out_ref[b] = (mid_ref[b].astype(F32) + nn(attended, wo_ref[...])).astype(BF16)
        deliver(b).start()
        return early

    at_first = places(0)
    fill(kca_ref, at_first)
    fill(kcb_ref, at_first)
    query_first = q_ref[0]
    bias_first = bias_of(0)
    lax.fori_loop(
        0,
        blocks,
        attend,
        tuple(score(kca_ref, query_first, pair, bias_first) for pair in (0, 1)),
        unroll=2,
    )

    def sent(c, carry):
        whole(rows_ref, c, go_sem, come_sem).wait_send()
        whole(ret_ref, c, back_sem, home_sem).wait_send()
        to_left(c).wait_send()
        to_right(c).wait_send()
        return carry

    lax.fori_loop(0, chunks, sent, 0)

    def delivered(b, carry):
        deliver(b).wait()
        return carry

    lax.fori_loop(0, blocks, delivered, 0)


def rotary_tables(tokens, head_dim):
    half = head_dim // 2
    freqs = np.power(np.float32(10000.0), -np.arange(half, dtype=np.float32) / np.float32(half))
    angle = np.arange(tokens, dtype=np.float32)[:, None] * freqs[None, :].astype(np.float32)
    angle = np.tile(angle.astype(np.float64), (1, BLOCK // half))
    return np.cos(angle).astype(np.float32), np.sin(angle).astype(np.float32)


def body(
    state_tokens,
    gain_time,
    query_time,
    key_time,
    value_time,
    output_time,
    gain_space,
    query_space,
    key_space,
    value_space,
    output_space,
    neighbours,
):
    tokens, width = state_tokens.shape[1:]
    frames = lax.axis_size("frame")
    slab = 2 * BLOCK // frames
    chunks = tokens // (frames * slab)
    blocks = tokens // BLOCK
    head_dim = width // HEADS
    cosine, sine = rotary_tables(tokens, head_dim)
    updated = pl.pallas_call(
        layer_kernel,
        out_shape=jax.ShapeDtypeStruct((tokens, width), BF16),
        in_specs=[pl.BlockSpec(memory_space=pltpu.SMEM)] + [pl.BlockSpec(memory_space=pltpu.HBM)] * 13,
        out_specs=pl.BlockSpec(memory_space=pltpu.HBM),
        scratch_shapes=[
            pltpu.VMEM((tokens, width), BF16),
            pltpu.VMEM((1, width), F32),
            pltpu.VMEM((width, width), BF16),
            pltpu.VMEM((width, width), BF16),
            pltpu.VMEM((width, width), BF16),
            pltpu.VMEM((width, width), BF16),
            pltpu.VMEM((1, width), F32),
            pltpu.VMEM((width, width), BF16),
            pltpu.VMEM((width, width), BF16),
            pltpu.VMEM((width, width), BF16),
            pltpu.VMEM((width, width), BF16),
            pltpu.VMEM((tokens, BLOCK), F32),
            pltpu.VMEM((tokens, BLOCK), F32),
            pltpu.SemaphoreType.DMA((13,)),
            pltpu.VMEM((blocks, BLOCK, width), BF16),
            pltpu.SemaphoreType.DMA((blocks,)),
            pltpu.VMEM((chunks, frames, slab, width), BF16),
            pltpu.VMEM((chunks, frames, slab, width), BF16),
            pltpu.VMEM((chunks, frames, slab, width), BF16),
            pltpu.VMEM((3 * blocks, BLOCK, width), BF16),
            pltpu.VMEM((blocks, BLOCK, width), BF16),
            pltpu.VMEM((blocks, BLOCK, width), BF16),
            pltpu.VMEM((3 * blocks, BLOCK, width), BF16),
            pltpu.VMEM((3 * blocks, HEADS // 2, 2 * head_dim + 16, BLOCK), BF16),
            pltpu.VMEM((width, 2 * width), BF16),
            pltpu.VMEM((width, 2 * width), BF16),
            pltpu.VMEM((width, width), BF16),
            pltpu.VMEM((width, width), BF16),
            pltpu.VMEM((NEIGHBOUR_COUNT * BLOCK, width), BF16),
            pltpu.VMEM((NEIGHBOUR_COUNT * BLOCK, width), BF16),
            pltpu.VMEM((HEADS // 2, NEIGHBOUR_COUNT * BLOCK, 2 * BLOCK), F32),
            pltpu.VMEM((width, BLOCK), F32),
        ]
        + [pltpu.SemaphoreType.DMA((chunks,))] * 8,
        compiler_params=pltpu.CompilerParams(
            vmem_limit_bytes=67043328, collective_id=1, has_side_effects=True
        ),
    )(
        neighbours,
        state_tokens.reshape(tokens, width),
        gain_time.reshape(1, width),
        query_time,
        key_time,
        value_time,
        output_time,
        gain_space.reshape(1, width),
        query_space,
        key_space,
        value_space,
        output_space,
        jnp.asarray(cosine),
        jnp.asarray(sine),
    )
    return updated.reshape(state_tokens.shape)


def solution(mesh):
    return jax.shard_map(
        body,
        mesh=mesh,
        in_specs=(P("frame", "tile", None),) + (P(),) * 10 + (P("tile", None),),
        out_specs=P("frame", "tile", None),
        check_vma=False,
    )
```

```python
import functools
import math

import jax
import jax.numpy as jnp
import numpy as np
from jax import lax
from jax.experimental import pallas as pl
from jax.experimental.pallas import tpu as pltpu
from jax.sharding import PartitionSpec as P

HEADS = 8
BLOCK = 128
NEIGHBOUR_COUNT = 9
EPS = 1e-05
ROT_PERIOD = 1024
NEG = -1e30
F32 = jnp.float32
BF16 = jnp.bfloat16
MESH = pl.DeviceIdType.MESH


def nt(a, b):
    return lax.dot_general(a, b, (((1,), (1,)), ((), ())), preferred_element_type=F32)


def nn(a, b):
    return lax.dot_general(a, b, (((1,), (0,)), ((), ())), preferred_element_type=F32)


def rms(values, gain):
    square_mean = jnp.mean(values * values, axis=-1, keepdims=True)
    return values * lax.rsqrt(square_mean + EPS) * gain


def head_pair(rows, pair, head_dim):
    lane_head = lax.broadcasted_iota(jnp.int32, rows.shape, 1) // head_dim
    zero = jnp.zeros_like(rows)
    return jnp.concatenate(
        [jnp.where(lane_head == 2 * pair + k, rows, zero) for k in range(2)], axis=0
    )


def pair_result(total, head_dim, count):
    inverse = 1.0 / total[2 * head_dim : 2 * head_dim + 1, :]
    scaled = total[: 2 * head_dim, :] * inverse
    return jnp.concatenate(
        [scaled[:head_dim, :count], scaled[head_dim:, count:]], axis=0
    )


def time_chunk(slots, gain, wq, wk, wv_t, same, scale, head_dim):
    frames, tokens, width = slots.shape
    step = tokens // 2
    normed = rms(slots.astype(F32), gain)
    rows = jnp.concatenate(
        [
            normed[:, k * step : (k + 1) * step].reshape(BLOCK, width).astype(BF16)
            for k in range(2)
        ],
        axis=0,
    )
    query = (nn(rows, wq) * scale).astype(BF16)
    key = nn(rows, wk).astype(BF16)
    value_t = nt(wv_t, rows).astype(BF16)
    ones = jnp.ones((16, BLOCK), BF16)
    units = [(k, pair) for k in range(2) for pair in range(HEADS // 2)]
    scores = {}
    for k, pair in units:
        part = slice(k * BLOCK, (k + 1) * BLOCK)
        scores[k, pair] = jnp.where(
            same, nt(key[part], head_pair(query[part], pair, head_dim)), NEG
        )
    weights = {
        unit: jnp.exp2(value - jnp.max(value, axis=0, keepdims=True)).astype(BF16)
        for unit, value in scores.items()
    }
    halves = []
    for k in range(2):
        parts = []
        for pair in range(HEADS // 2):
            low = 2 * pair * head_dim
            held = jnp.concatenate(
                [value_t[low : low + 2 * head_dim, k * BLOCK : (k + 1) * BLOCK], ones], axis=0
            )
            parts.append(pair_result(nn(held, weights[k, pair]), head_dim, BLOCK))
        halves.append(jnp.concatenate(parts, axis=0).T.reshape(frames, step, width))
    return jnp.concatenate(halves, axis=1)


def swapped(weight):
    wide = weight.astype(F32)
    width = wide.shape[1]
    half = width // HEADS // 2
    lane = lax.broadcasted_iota(jnp.int32, wide.shape, 1)
    ahead = pltpu.roll(wide, width - half, 1)
    behind = pltpu.roll(wide, half, 1)
    return jnp.where(lane % (2 * half) < half, -ahead, behind).astype(BF16)


def layer_kernel(
    nbr_ref,
    state_hbm,
    gain_t_hbm,
    wqt_hbm,
    wkt_hbm,
    wvt_in_hbm,
    wt_hbm,
    gain_hbm,
    wq_hbm,
    wk_hbm,
    wv_hbm,
    wo_hbm,
    cos_hbm,
    sin_hbm,
    out_hbm,
    state_ref,
    gain_t_ref,
    wqt_ref,
    wkt_ref,
    wvt_in_ref,
    wt_ref,
    gain_ref,
    wq_ref,
    wk_ref,
    wv_ref,
    wo_ref,
    cos_ref,
    sin_ref,
    load_sem,
    out_ref,
    out_sem,
    rows_ref,
    attn_ref,
    ret_ref,
    norm_ref,
    mid_ref,
    q_ref,
    k_ref,
    v_ref,
    wq2_ref,
    wk2_ref,
    wvt_ref,
    wvtt_ref,
    kca_ref,
    kcb_ref,
    s_ref,
    att_ref,
    go_sem,
    come_sem,
    back_sem,
    home_sem,
    send_l,
    recv_l,
    send_r,
    recv_r,
):
    blocks = mid_ref.shape[0]
    width = state_ref.shape[-1]
    sources = (state_hbm, gain_t_hbm, wqt_hbm, wkt_hbm, wvt_in_hbm, wt_hbm, gain_hbm, wq_hbm, wk_hbm, wv_hbm, wo_hbm, cos_hbm, sin_hbm)
    targets = (state_ref, gain_t_ref, wqt_ref, wkt_ref, wvt_in_ref, wt_ref, gain_ref, wq_ref, wk_ref, wv_ref, wo_ref, cos_ref, sin_ref)
    loads = [
        pltpu.make_async_copy(source, target, load_sem.at[i])
        for i, (source, target) in enumerate(zip(sources, targets))
    ]
    head_dim = width // HEADS
    scale = math.log2(math.e) / math.sqrt(head_dim)
    chunks, frames, slab, _ = rows_ref.shape
    half = frames // 2
    per = blocks // chunks
    tile = lax.axis_index("tile")
    tiles = lax.axis_size("tile")
    left = lax.rem(tile + tiles - 1, tiles)
    right = lax.rem(tile + 1, tiles)
    me = lax.axis_index("frame")
    my_side = me // half
    my_place = lax.rem(me, half)

    def peer_at(k):
        return lax.rem(my_side + k // half, 2) * half + lax.rem(my_place + lax.rem(k, half), half)

    def mirror(k):
        return (k // half) * half + lax.rem(half - lax.rem(k, half), half)

    barrier = pltpu.get_barrier_semaphore()

    def greet(k, carry):
        pl.semaphore_signal(
            barrier, inc=1, device_id={"frame": peer_at(k)}, device_id_type=MESH
        )
        return carry

    lax.fori_loop(1, frames, greet, 0)
    for peer in (left, right):
        pl.semaphore_signal(barrier, inc=1, device_id={"tile": peer}, device_id_type=MESH)

    def go(c, k):
        at = pl.ds(pl.multiple_of((c * frames + peer_at(k)) * slab, slab), slab)
        return pltpu.make_async_remote_copy(
            src_ref=state_hbm.at[at, :],
            dst_ref=rows_ref.at[c, mirror(k)],
            send_sem=go_sem.at[c],
            recv_sem=come_sem.at[c],
            device_id={"frame": peer_at(k)},
            device_id_type=MESH,
        )

    def back(c, k):
        return pltpu.make_async_remote_copy(
            src_ref=attn_ref.at[c, k],
            dst_ref=ret_ref.at[c, me],
            send_sem=back_sem.at[c],
            recv_sem=home_sem.at[c],
            device_id={"frame": peer_at(k)},
            device_id_type=MESH,
        )

    def whole(ref, c, send_sem, recv_sem):
        return pltpu.make_async_remote_copy(
            src_ref=ref.at[c, pl.ds(0, frames - 1)],
            dst_ref=ref.at[c, pl.ds(0, frames - 1)],
            send_sem=send_sem.at[c],
            recv_sem=recv_sem.at[c],
            device_id={"frame": peer_at(1)},
            device_id_type=MESH,
        )

    def to_left(c):
        return pltpu.make_async_remote_copy(
            src_ref=norm_ref.at[pl.ds(blocks + per * c, per)],
            dst_ref=norm_ref.at[pl.ds(2 * blocks + per * c, per)],
            send_sem=send_l.at[c],
            recv_sem=recv_l.at[c],
            device_id={"tile": left},
            device_id_type=MESH,
        )

    def to_right(c):
        return pltpu.make_async_remote_copy(
            src_ref=norm_ref.at[pl.ds(blocks + per * c, per)],
            dst_ref=norm_ref.at[pl.ds(per * c, per)],
            send_sem=send_r.at[c],
            recv_sem=recv_r.at[c],
            device_id={"tile": right},
            device_id_type=MESH,
        )

    for load in loads:
        load.start()
    pl.semaphore_wait(barrier, frames + 1)

    def leave(c, carry):
        def one(i, inner):
            go(c, frames - 1 - i).start()
            return inner

        return lax.fori_loop(0, frames - 1, one, carry, unroll=5)

    lax.fori_loop(0, chunks, leave, 0)

    for load in loads:
        load.wait()

    def stay(c, carry):
        at = pl.ds(pl.multiple_of((c * frames + me) * slab, slab), slab)
        rows_ref[c, 0] = state_ref[at, :]
        return carry

    lax.fori_loop(0, chunks, stay, 0)
    wvtt_ref[...] = wvt_in_ref[...].astype(F32).T.astype(BF16)
    wq2_ref[:, :width] = wq_ref[...]
    wq2_ref[:, width:] = swapped(wq_ref[...])
    wk2_ref[:, :width] = wk_ref[...]
    wk2_ref[:, width:] = swapped(wk_ref[...])
    wvt_ref[...] = wv_ref[...].astype(F32).T.astype(BF16)


    row = lax.broadcasted_iota(jnp.int32, (BLOCK, 2 * BLOCK), 0)
    column = lax.broadcasted_iota(jnp.int32, (BLOCK, 2 * BLOCK), 1)
    step = slab // 2
    same = (row % step) == (column % step)

    def over_time(c, carry):
        whole(rows_ref, c, go_sem, come_sem).wait_recv()
        attended = time_chunk(
            rows_ref[c],
            gain_t_ref[...],
            wqt_ref[...],
            wkt_ref[...],
            wvtt_ref[...],
            same,
            scale,
            head_dim,
        )
        attn_ref[c] = attended.astype(BF16)

        def one(i, inner):
            back(c, frames - 1 - i).start()
            return inner

        lax.fori_loop(0, frames - 1, one, 0, unroll=5)
        ret_ref[c, me] = attn_ref[c, 0]
        return carry

    lax.fori_loop(0, chunks, over_time, 0)

    def turn(rows, weight_ref, j):
        at = pl.ds(pl.multiple_of(j * BLOCK, BLOCK), 2 * BLOCK)
        cosine = jnp.concatenate([cos_ref[at, :]] * 2, axis=1)
        sine = jnp.concatenate([sin_ref[at, :]] * 2, axis=1)
        both = nn(rows, weight_ref[...])
        return both[:, :width] * cosine + both[:, width:] * sine

    ones = jnp.ones((16, BLOCK), BF16)

    def key_value(g, j):
        rows = norm_ref[pl.ds(g, 2)].reshape(2 * BLOCK, width)
        k_ref[pl.ds(g, 2)] = turn(rows, wk2_ref, j).astype(BF16).reshape(2, BLOCK, width)
        value_t = nt(wvt_ref[...], rows).astype(BF16)
        for pair in range(HEADS // 2):
            low = 2 * pair * head_dim
            for k in range(2):
                v_ref[g + k, pair] = jnp.concatenate(
                    [value_t[low : low + 2 * head_dim, k * BLOCK : (k + 1) * BLOCK], ones], axis=0
                )

    gain = gain_ref[...]

    def own(c, carry):
        j = per * c
        whole(ret_ref, c, back_sem, home_sem).wait_recv()
        at = pl.ds(pl.multiple_of(c * frames * slab, frames * slab), frames * slab)
        returned = ret_ref[c].reshape(frames * slab, width)
        mid = (state_ref[at, :].astype(F32) + nn(returned, wt_ref[...])).astype(BF16)
        mid_ref[pl.ds(j, per)] = mid.reshape(per, BLOCK, width)
        rows = rms(mid.astype(F32), gain).astype(BF16)
        norm_ref[pl.ds(blocks + j, per)] = rows.reshape(per, BLOCK, width)
        to_left(c).start()
        to_right(c).start()
        query = (turn(rows, wq2_ref, j) * scale).astype(BF16)
        q_ref[pl.ds(j, per)] = query.reshape(per, BLOCK, width)
        key_value(blocks + j, j)
        return carry

    lax.fori_loop(0, chunks, own, 0)

    first = (tile - 1) * blocks
    total_blocks = tiles * blocks

    def place(b, m):
        entry = nbr_ref[b, m]
        offset = entry - first
        offset = jnp.where(offset < 0, offset + total_blocks, offset)
        offset = jnp.where(offset >= total_blocks, offset - total_blocks, offset)
        offset = jnp.minimum(offset, 3 * blocks - 1)
        return jnp.where(entry < 0, blocks + b, offset)

    def places(b):
        return [place(b, m) for m in range(NEIGHBOUR_COUNT)]

    last_rows = (NEIGHBOUR_COUNT - 1) * BLOCK

    def bias_of(b):
        return jnp.where(nbr_ref[b, NEIGHBOUR_COUNT - 1] < 0, NEG, 0.0).astype(F32)

    def fill(kc_ref, at):
        for m in range(NEIGHBOUR_COUNT):
            kc_ref[m * BLOCK : (m + 1) * BLOCK, :] = k_ref[at[m]]

    def score(kc_ref, query, pair, bias):
        scores = nt(kc_ref[...], head_pair(query, pair, head_dim))
        tail = scores[last_rows:] + bias
        s_ref[pair, :last_rows, :] = scores[:last_rows]
        s_ref[pair, last_rows:, :] = tail
        return jnp.maximum(
            jnp.max(scores[:last_rows], axis=0, keepdims=True),
            jnp.max(tail, axis=0, keepdims=True),
        )

    def weigh(at, pair, top):
        weights = jnp.exp2(s_ref[pair] - top).astype(BF16)
        held = jnp.concatenate([v_ref[g, pair] for g in at], axis=1)
        low = 2 * pair * head_dim
        att_ref[low : low + 2 * head_dim, :] = pair_result(nn(held, weights), head_dim, BLOCK)

    def arrive(c, carry):
        to_left(c).wait_recv()
        key_value(2 * blocks + per * c, per * c)
        to_right(c).wait_recv()
        key_value(per * c, per * c)
        return carry

    lax.fori_loop(0, chunks, arrive, 0)

    def deliver(b):
        at = pl.ds(pl.multiple_of(b * BLOCK, BLOCK), BLOCK)
        return pltpu.make_async_copy(out_ref.at[b], out_hbm.at[at, :], out_sem.at[b])

    def attend(b, tops):
        here = places(b)
        after = jnp.minimum(b + 1, blocks - 1)
        there = places(after)
        query = q_ref[b]
        bias = bias_of(b)
        fill(kca_ref, there)
        query_after = q_ref[after]
        bias_after = bias_of(after)
        late = [score(kcb_ref, query, 2, bias)]
        weigh(here, 0, tops[0])
        early = [score(kca_ref, query_after, 0, bias_after)]
        late.append(score(kcb_ref, query, 3, bias))
        fill(kcb_ref, there)
        weigh(here, 1, tops[1])
        early.append(score(kca_ref, query_after, 1, bias_after))
        weigh(here, 2, late[0])
        weigh(here, 3, late[1])
        early = tuple(early)
        attended = att_ref[...].T.astype(BF16)
        out_ref[b] = (mid_ref[b].astype(F32) + nn(attended, wo_ref[...])).astype(BF16)
        deliver(b).start()
        return early

    at_first = places(0)
    fill(kca_ref, at_first)
    fill(kcb_ref, at_first)
    query_first = q_ref[0]
    bias_first = bias_of(0)
    lax.fori_loop(
        0,
        blocks,
        attend,
        tuple(score(kca_ref, query_first, pair, bias_first) for pair in (0, 1)),
        unroll=2,
    )

    def sent(c, carry):
        whole(rows_ref, c, go_sem, come_sem).wait_send()
        whole(ret_ref, c, back_sem, home_sem).wait_send()
        to_left(c).wait_send()
        to_right(c).wait_send()
        return carry

    lax.fori_loop(0, chunks, sent, 0)

    def delivered(b, carry):
        deliver(b).wait()
        return carry

    lax.fori_loop(0, blocks, delivered, 0)


def rotary_tables(tokens, head_dim):
    half = head_dim // 2
    freqs = np.power(np.float32(10000.0), -np.arange(half, dtype=np.float32) / np.float32(half))
    angle = np.arange(tokens, dtype=np.float32)[:, None] * freqs[None, :].astype(np.float32)
    angle = np.tile(angle.astype(np.float64), (1, BLOCK // half))
    return np.cos(angle).astype(np.float32), np.sin(angle).astype(np.float32)


def body(
    state_tokens,
    gain_time,
    query_time,
    key_time,
    value_time,
    output_time,
    gain_space,
    query_space,
    key_space,
    value_space,
    output_space,
    neighbours,
):
    tokens, width = state_tokens.shape[1:]
    frames = lax.axis_size("frame")
    slab = 2 * BLOCK // frames
    chunks = tokens // (frames * slab)
    blocks = tokens // BLOCK
    head_dim = width // HEADS
    cosine, sine = rotary_tables(tokens, head_dim)
    updated = pl.pallas_call(
        layer_kernel,
        out_shape=jax.ShapeDtypeStruct((tokens, width), BF16),
        in_specs=[pl.BlockSpec(memory_space=pltpu.SMEM)] + [pl.BlockSpec(memory_space=pltpu.HBM)] * 13,
        out_specs=pl.BlockSpec(memory_space=pltpu.HBM),
        scratch_shapes=[
            pltpu.VMEM((tokens, width), BF16),
            pltpu.VMEM((1, width), F32),
            pltpu.VMEM((width, width), BF16),
            pltpu.VMEM((width, width), BF16),
            pltpu.VMEM((width, width), BF16),
            pltpu.VMEM((width, width), BF16),
            pltpu.VMEM((1, width), F32),
            pltpu.VMEM((width, width), BF16),
            pltpu.VMEM((width, width), BF16),
            pltpu.VMEM((width, width), BF16),
            pltpu.VMEM((width, width), BF16),
            pltpu.VMEM((tokens, BLOCK), F32),
            pltpu.VMEM((tokens, BLOCK), F32),
            pltpu.SemaphoreType.DMA((13,)),
            pltpu.VMEM((blocks, BLOCK, width), BF16),
            pltpu.SemaphoreType.DMA((blocks,)),
            pltpu.VMEM((chunks, frames, slab, width), BF16),
            pltpu.VMEM((chunks, frames, slab, width), BF16),
            pltpu.VMEM((chunks, frames, slab, width), BF16),
            pltpu.VMEM((3 * blocks, BLOCK, width), BF16),
            pltpu.VMEM((blocks, BLOCK, width), BF16),
            pltpu.VMEM((blocks, BLOCK, width), BF16),
            pltpu.VMEM((3 * blocks, BLOCK, width), BF16),
            pltpu.VMEM((3 * blocks, HEADS // 2, 2 * head_dim + 16, BLOCK), BF16),
            pltpu.VMEM((width, 2 * width), BF16),
            pltpu.VMEM((width, 2 * width), BF16),
            pltpu.VMEM((width, width), BF16),
            pltpu.VMEM((width, width), BF16),
            pltpu.VMEM((NEIGHBOUR_COUNT * BLOCK, width), BF16),
            pltpu.VMEM((NEIGHBOUR_COUNT * BLOCK, width), BF16),
            pltpu.VMEM((HEADS // 2, NEIGHBOUR_COUNT * BLOCK, 2 * BLOCK), F32),
            pltpu.VMEM((width, BLOCK), F32),
        ]
        + [pltpu.SemaphoreType.DMA((chunks,))] * 8,
        compiler_params=pltpu.CompilerParams(
            vmem_limit_bytes=67043328, collective_id=1, has_side_effects=True
        ),
    )(
        neighbours,
        state_tokens.reshape(tokens, width),
        gain_time.reshape(1, width),
        query_time,
        key_time,
        value_time,
        output_time,
        gain_space.reshape(1, width),
        query_space,
        key_space,
        value_space,
        output_space,
        jnp.asarray(cosine),
        jnp.asarray(sine),
    )
    return updated.reshape(state_tokens.shape)


def solution(mesh):
    return jax.shard_map(
        body,
        mesh=mesh,
        in_specs=(P("frame", "tile", None),) + (P(),) * 10 + (P("tile", None),),
        out_specs=P("frame", "tile", None),
        check_vma=False,
    )
```
